256 devices in a mesh: row: 8 (over y, core), col: 32 (over z, x).
Axes of the slice: x: 4, y: 4, z: 8, core: 2. Of those that a mesh axis runs over, the one named last changes fastest.
Arguments:
- modes: float32 [48, 2, 64, 4096], P(None, None, 'row', 'col'), may hold values from -25 to 25
- mean_flow: float32 [2, 64, 4096], P(None, 'row', 'col'), may hold values from -5 to 5
- seeds: int32 [32768, 48], P(('row', 'col')), may hold values from 0 to 4095
- amplitudes: float32 [48], replicated, may hold values from 0.5 to 2
- water_mask: int32 [64, 4096], P('row', 'col'), may hold values 0 or 1
Outputs:
- new_modes: float32 [48, 2, 64, 4096], P(None, None, 'row', 'col')
- new_coeffs: float32 [32768, 48], P(('row', 'col'))
The draws below stay inside these ranges and needn't reach their ends.
Inputs may be any that keep to these rules, and one draw needn't show every extreme that they name: `water_mask`: 1 marks a water cell, 0 a land cell.
All inputs are finite; a program needn't handle non-finite values. No bound on the sum of `water_mask` on one device may be relied on, other than what follows from the above.
Results may differ from the reference program's by a relative error of at most 0.0003.
Values sent between devices are 32-bit elements; how exact they have to be, the bound alone decides.
A program may use at most 128 MiB of HBM per device.

```python
import math
import jax
import jax.numpy as jnp
from jax import lax

S = 48
NX = 64
NY = 4096
R = 32768


def lattice_field(key, count):
    subkeys = jax.random.split(key, 5)
    x_cells = jnp.arange(NX, dtype=jnp.float32)[:, None]
    y_cells = jnp.arange(NY, dtype=jnp.float32)[None, :]
    wave_x = jax.random.randint(subkeys[0], (count, 2, 3), -2, 3).astype(jnp.float32)
    wave_y = jax.random.randint(subkeys[1], (count, 2, 3), -2, 3).astype(jnp.float32)
    phases = jax.random.uniform(subkeys[2], (count, 2, 3), jnp.float32, -math.pi, math.pi)
    wave_amp = jax.random.uniform(subkeys[3], (count, 2, 3), jnp.float32, -1.0, 1.0)
    smooth = jnp.zeros((count, 2, NX, NY), jnp.float32)
    for number in range(3):
        argument = 2.0 * math.pi / 32.0 * (wave_x[:, :, number, None, None] * x_cells + wave_y[:, :, number, None, None] * y_cells) + phases[:, :, number, None, None]
        smooth = smooth + wave_amp[:, :, number, None, None] * jnp.cos(argument)
    rough_part = jnp.clip(jax.random.normal(subkeys[4], (count, 2, NX, NY), jnp.float32), -4.0, 4.0)
    return smooth + 0.5 * rough_part


def draw_modes(key, part):
    own_part = lattice_field(jax.random.fold_in(key, 11), S)
    shared = lattice_field(jax.random.fold_in(key, 12), 1)
    loadings = jax.random.uniform(jax.random.fold_in(key, 13), (S, 1, 1, 1), jnp.float32, 0.5, 1.5)
    field = own_part + loadings * shared
    return field


def draw_mean_flow(key, part):
    return lattice_field(jax.random.fold_in(key, 21), 1)[0]


def set_ends(entries, key, least, top_value):
    index_at = [jax.random.randint(jax.random.fold_in(key, axis), (), 0, length) for axis, length in enumerate(entries.shape)]
    longest = entries.shape.index(max(entries.shape))
    next_to = index_at[:longest] + [(index_at[longest] + 1) % entries.shape[longest]] + index_at[longest + 1:]
    return entries.at[tuple(index_at)].set(least).at[tuple(next_to)].set(top_value)


def setup_inputs(seed: int = 0) -> dict:
    streams_of = jax.random.split(jax.random.key(seed), 6)
    return {
        "modes": draw_modes(jax.random.fold_in(streams_of[5], 71), 0),
        "mean_flow": draw_mean_flow(jax.random.fold_in(streams_of[5], 71), 0),
        "seeds": set_ends(jax.random.randint(streams_of[2], (R, S), 0, 4096), jax.random.fold_in(streams_of[2], 1), 0, 4095).astype(jnp.int32),
        "amplitudes": jnp.clip(jnp.exp(jax.random.uniform(streams_of[3], (S,), jnp.float32, math.log(0.5), math.log(2.0))), 0.5, 2.0),
        "water_mask": set_ends((jax.random.randint(streams_of[4], (NX, NY), 0, 8) < 7).astype(jnp.int32), jax.random.fold_in(streams_of[4], 1), 0, 1),
    }


TIME_STEP = 0.25
VISCOUS = 0.2
PRECISE = lax.Precision.HIGHEST

def matmul(left_side, right_side):
    return jnp.dot(left_side.astype(jnp.float32), right_side.astype(jnp.float32), precision=PRECISE, preferred_element_type=jnp.float32)

def matmul_nt(left_side, right_side):
    return lax.dot_general(left_side.astype(jnp.float32), right_side.astype(jnp.float32), (((1,), (1,)), ((), ())), precision=PRECISE, preferred_element_type=jnp.float32)

def factor_solve(factor, right_side):
    lower_part = lax.linalg.triangular_solve(factor, right_side, left_side=True, lower=True)
    return lax.linalg.triangular_solve(factor, lower_part, left_side=True, lower=True, transpose_a=True)

def raw_coeffs(seeds, amplitudes, first_row, row_total):
    phases = seeds.astype(jnp.float32) * (3.0 * math.pi / 8192.0)
    row_ids = (first_row + jnp.arange(seeds.shape[0], dtype=jnp.int32)).astype(jnp.float32)
    strength = 0.5 + row_ids / row_total
    return strength[:, None] * amplitudes[None, :] * (jnp.cos(phases) + 0.5 * jnp.cos(2.0 * phases))

def pair_products(coeffs):
    return (coeffs[:, :, None] * coeffs[:, None, :]).reshape(coeffs.shape[0], -1)

def derivatives(padded):
    along_x = 0.5 * (padded[:, :, 2:, 1:-1] - padded[:, :, :-2, 1:-1])
    along_y = 0.5 * (padded[:, :, 1:-1, 2:] - padded[:, :, 1:-1, :-2])
    return (along_x, along_y)

def transport_term(advecting_velocity, gradient_east, gradient_north):
    return advecting_velocity[..., 0:1, :, :] * gradient_east + advecting_velocity[..., 1:2, :, :] * gradient_north

def reference(modes, mean_flow, seeds, amplitudes, water_mask):
    mode_count = modes.shape[0]
    uncentered = raw_coeffs(seeds, amplitudes, 0, R)
    coeffs = uncentered - jnp.sum(uncentered, axis=0) / R
    pair_terms = pair_products(coeffs)
    covariance = matmul(coeffs.T, coeffs) / R
    third_moment = matmul(coeffs.T, pair_terms) / R
    weight_map = factor_solve(jnp.linalg.cholesky(covariance), third_moment)
    weight_cube = weight_map.reshape(mode_count, mode_count, mode_count)
    stacked_fields = jnp.concatenate([modes, mean_flow[None]], axis=0)
    padded = jnp.pad(stacked_fields, ((0, 0), (0, 0), (1, 1), (1, 1)))
    grad_x, grad_y = derivatives(padded)
    water_cells = water_mask.astype(jnp.float32)
    weight_scale = 1.0 / (2.0 * NX * NY)
    mode_grad_x = grad_x[:mode_count]
    mode_grad_y = grad_y[:mode_count]
    linear = -(transport_term(mean_flow, mode_grad_x, mode_grad_y) + transport_term(modes, grad_x[mode_count:], grad_y[mode_count:]))
    flat_modes = modes.reshape(mode_count, -1)
    weighted = (modes * (water_cells * weight_scale)).reshape(mode_count, -1)
    gram_matrix = matmul_nt(weighted, flat_modes)
    linear_projection = matmul_nt(weighted, linear.reshape(mode_count, -1))

    def advance(nonlinear, position):
        single = lax.dynamic_index_in_dim(modes, position, 0, keepdims=False)
        pair_field = (single[0:1] * mode_grad_x + single[1:2] * mode_grad_y).reshape(mode_count, -1)
        column = -matmul_nt(weighted, pair_field)
        weight_slice = lax.dynamic_index_in_dim(weight_cube, position, 1, keepdims=False)
        return (nonlinear + matmul(weight_slice, pair_field), column)
    nonlinear, columns = lax.scan(advance, jnp.zeros_like(flat_modes), jnp.arange(mode_count, dtype=jnp.int32))
    tensor = jnp.transpose(columns, (1, 0, 2)).reshape(mode_count, -1)
    forcing = water_cells * (linear - nonlinear.reshape(modes.shape))
    projected = matmul_nt(weighted, forcing.reshape(mode_count, -1))
    factor = jnp.linalg.cholesky(gram_matrix)
    solved = factor_solve(factor, projected)
    correction = matmul(solved.T, flat_modes).reshape(modes.shape)
    half_step = water_cells * (modes + TIME_STEP * (forcing - correction))
    beside_all = jnp.pad(half_step, ((0, 0), (0, 0), (1, 1), (1, 1)))
    laplace_term = beside_all[:, :, 2:, 1:-1] + beside_all[:, :, :-2, 1:-1] + beside_all[:, :, 1:-1, 2:] + beside_all[:, :, 1:-1, :-2] - 4.0 * half_step
    new_modes = water_cells * (half_step + VISCOUS * laplace_term)
    drift = matmul(coeffs, linear_projection.T) + matmul(pair_terms - covariance.reshape(1, -1), tensor.T)
    change = factor_solve(factor, drift.T).T
    new_coeffs = coeffs + TIME_STEP * change
    return (new_modes, new_coeffs)
```

```python
import math

import jax
import jax.numpy as jnp
from jax import lax
from jax.experimental import pallas as pl
from jax.experimental.pallas import tpu as pltpu
from jax.sharding import PartitionSpec as P

F32 = jnp.float32
BF16 = jnp.bfloat16
MESH = pl.DeviceIdType.MESH
HIGHEST = lax.Precision.HIGHEST

S = 48
R = 32768
CELLS = 2.0 * 64 * 4096
STEP = 0.25
VISCOUS = 0.2
ROWS, COLS, ALONG_X = 8, 32, 4
GROUP = ROWS * ALONG_X
DEEP = COLS // ALONG_X
CHUNK = 16
REGION = GROUP * CHUNK
PAIRS = 1176
WIDE = 1280
NT = (((1,), (1,)), ((), ()))


def split(value):
    high = value.astype(BF16)
    return high, (value - high.astype(F32)).astype(BF16)


def dot(a, b):
    return jnp.dot(a, b, preferred_element_type=F32)


def dot_nt(a, b):
    return lax.dot_general(a, b, NT, preferred_element_type=F32)


def exact(a, b):
    return jnp.dot(a, b, precision=HIGHEST, preferred_element_type=F32)


def exact_nt(a, b):
    return lax.dot_general(a, b, NT, precision=HIGHEST, preferred_element_type=F32)


def tall(value):
    return jnp.concatenate([value, jnp.zeros((128 - S, 128), F32)], axis=0)


def kernel(
    modes, mean, seeds, amps, water, new_modes, new_coeffs,
    base, both, grad_x, grad_y, back, weighted, pair_high, pair_low, side_high, side_low,
    square, coeffs, pair_coeffs, moments, tensor, cube, cube_split, pair_cov,
    cov_inv, gram_inv, half,
    part_a, deep_a, mine_a, total_a, part_b, deep_b, mine_b, total_b,
    up_out, down_out, left_out, right_out, up_in, down_in, left_in, right_in,
    up_out2, down_out2, left_out2, right_out2, up_in2, down_in2, left_in2, right_in2,
    halo_send, halo_recv, sum_send, sum_recv,
):
    row = lax.axis_index("row")
    col = lax.axis_index("col")
    along_x = lax.rem(col, ALONG_X)
    plane = lax.div(col, ALONG_X)
    place = row * ALONG_X + along_x
    above = lax.rem(row + ROWS - 1, ROWS)
    below = lax.rem(row + 1, ROWS)
    left = lax.rem(col + COLS - 1, COLS)
    right = lax.rem(col + 1, COLS)

    def member(offset):
        other = lax.rem(place + offset, GROUP)
        return other, (lax.div(other, ALONG_X), plane * ALONG_X + lax.rem(other, ALONG_X))

    def deep(offset):
        return (row, lax.rem(plane + offset, DEEP) * ALONG_X + along_x)

    barrier = pltpu.get_barrier_semaphore()

    def greet_plane(offset, carry):
        pl.semaphore_signal(barrier, inc=1, device_id=member(offset)[1], device_id_type=MESH)
        return carry

    def greet_deep(offset, carry):
        pl.semaphore_signal(barrier, inc=1, device_id=deep(offset), device_id_type=MESH)
        return carry

    lax.fori_loop(1, GROUP, greet_plane, 0)
    lax.fori_loop(1, DEEP, greet_deep, 0)
    pl.semaphore_signal(barrier, inc=1, device_id=(row, left), device_id_type=MESH)
    pl.semaphore_signal(barrier, inc=1, device_id=(row, right), device_id_type=MESH)

    lane = lax.broadcasted_iota(jnp.int32, (S, 128), 1)
    lane1 = lax.broadcasted_iota(jnp.int32, (1, 128), 1)
    sub = lax.broadcasted_iota(jnp.int32, (S, 128), 0)
    sub8 = lax.broadcasted_iota(jnp.int32, (8, 128), 0)

    def copies(outs, ins, first):
        targets = ((above, col), (below, col), (row, left), (row, right))
        arrivals = (ins[1], ins[0], ins[3], ins[2])
        return [
            pltpu.make_async_remote_copy(
                src_ref=outs[k],
                dst_ref=arrivals[k],
                send_sem=halo_send.at[first + k],
                recv_sem=halo_recv.at[first + k],
                device_id=targets[k],
                device_id_type=MESH,
            )
            for k in range(4)
        ]

    def plane_start(source, parts, sems):
        def send(offset, carry):
            other, device = member(offset)
            pltpu.make_async_remote_copy(
                src_ref=source.at[pl.ds(pl.multiple_of(other * CHUNK, CHUNK), CHUNK)],
                dst_ref=parts.at[pl.ds(pl.multiple_of((offset - 1) * CHUNK, CHUNK), CHUNK)],
                send_sem=sum_send.at[sems],
                recv_sem=sum_recv.at[sems],
                device_id=device,
                device_id_type=MESH,
            ).start()
            return carry

        lax.fori_loop(1, GROUP, send, 0)

    def deep_start(source, parts, mine, deeper, sems):
        pltpu.make_async_copy(parts, parts, sum_recv.at[sems]).wait()
        value = source[pl.ds(pl.multiple_of(place * CHUNK, CHUNK), CHUNK), :]
        for k in range(GROUP - 1):
            value = value + parts[k * CHUNK : (k + 1) * CHUNK, :]
        mine[0:CHUNK, :] = value

        def send(offset, carry):
            pltpu.make_async_remote_copy(
                src_ref=mine.at[pl.ds(0, CHUNK)],
                dst_ref=deeper.at[pl.ds(pl.multiple_of((offset - 1) * CHUNK, CHUNK), CHUNK)],
                send_sem=sum_send.at[sems + 1],
                recv_sem=sum_recv.at[sems + 1],
                device_id=deep(offset),
                device_id_type=MESH,
            ).start()
            return carry

        lax.fori_loop(1, DEEP, send, 0)

    def gather_start(mine, deeper, total, sems):
        pltpu.make_async_copy(deeper, deeper, sum_recv.at[sems + 1]).wait()
        value = mine[0:CHUNK, :]
        for k in range(DEEP - 1):
            value = value + deeper[k * CHUNK : (k + 1) * CHUNK, :]
        mine[CHUNK : 2 * CHUNK, :] = value
        own = pl.ds(pl.multiple_of(place * CHUNK, CHUNK), CHUNK)
        total[own, :] = value

        def send(offset, carry):
            pltpu.make_async_remote_copy(
                src_ref=mine.at[pl.ds(CHUNK, CHUNK)],
                dst_ref=total.at[own],
                send_sem=sum_send.at[sems + 2],
                recv_sem=sum_recv.at[sems + 2],
                device_id=member(offset)[1],
                device_id_type=MESH,
            ).start()
            return carry

        lax.fori_loop(1, GROUP, send, 0)

    def gather_wait(parts, sems):
        pltpu.make_async_copy(parts, parts, sum_recv.at[sems + 2]).wait()

    def sums_sent(parts, deeper, sems):
        pltpu.make_async_copy(parts, parts, sum_send.at[sems]).wait()
        pltpu.make_async_copy(deeper, deeper, sum_send.at[sems + 1]).wait()
        pltpu.make_async_copy(parts, parts, sum_send.at[sems + 2]).wait()

    side_high[...] = jnp.zeros((128, 2048), BF16)
    side_low[...] = jnp.zeros((128, 2048), BF16)
    first_column = jnp.zeros((56, 128), F32)
    last_column = jnp.zeros((56, 128), F32)
    lane56 = lax.broadcasted_iota(jnp.int32, (56, 128), 1)
    for t in range(16):
        s = t % 8
        cells = slice(t * 128, (t + 1) * 128)
        field = modes[pl.ds(t, S, stride=16), :]
        drift_row = jnp.where(sub8 == 0, jnp.broadcast_to(mean[t : t + 1, :], (8, 128)), 0.0)
        block = jnp.concatenate([field, drift_row], axis=0)
        base[t] = block
        both[t, 0:S, :] = field
        both[t, S : S + 24, :] = field[0:24]
        weight = water[s : s + 1, :].astype(F32) * (-1.0 / CELLS)
        high, low = split(field * weight)
        weighted[0:S, cells] = high
        weighted[S : 2 * S, cells] = low
        high, low = split(field)
        side_high[64 : 64 + S, cells] = high
        side_low[64 : 64 + S, cells] = low
        shifted = pltpu.roll(block, t, 1) if t else block
        first_column = jnp.where(lane56 == t, shifted, first_column)
        last_column = jnp.where(lane56 == t, pltpu.roll(block, t + 1, 1), last_column)
        if s == 0:
            up_out[t // 8] = block
        if s == 7:
            down_out[t // 8] = block
    left_out[...] = first_column
    right_out[...] = last_column

    pl.semaphore_wait(barrier, GROUP - 1 + DEEP - 1 + 2)
    halo = copies(
        (up_out, down_out, left_out, right_out), (up_in, down_in, left_in, right_in), 0
    )
    for copy in halo:
        copy.start()

    phase = seeds[...].astype(F32) * (3.0 * math.pi / 8192.0)
    wave = jnp.cos(phase)
    number = (row * COLS + col) * 128 + lax.broadcasted_iota(jnp.int32, (128, S), 0)
    strength = 0.5 + number.astype(F32) * (1.0 / R)
    square[...] = jnp.zeros((128, 128), F32)
    square[:, 0:S] = strength * amps[...] * (wave + (wave * wave - 0.5))
    raw = square[...].T[0:S]

    def pair_up(values, ones):
        coeffs[0:S, :] = values
        coeffs[S : S + 24, :] = values[0:24]
        for d in range(24):
            pair_coeffs[d * S : (d + 1) * S, :] = values * coeffs[d : d + S, :]
        pair_coeffs[1152:PAIRS, :] = values[0:24] * coeffs[24:48, :]
        pair_coeffs[PAIRS : PAIRS + S, :] = values
        pair_coeffs[PAIRS + S : WIDE, :] = jnp.zeros((WIDE - PAIRS - S, 128), F32)
        if ones:
            pair_coeffs[1272:1280, :] = jnp.where(sub8 == 0, 1.0, 0.0)

    pair_up(raw, True)
    for lb in range(5):
        out = exact_nt(raw, pair_coeffs[lb * 256 : (lb + 1) * 256, :])
        moments[lb * 96 : lb * 96 + S, :] = out[:, 0:128]
        moments[lb * 96 + S : lb * 96 + 96, :] = out[:, 128:256]
    gram = dot_nt(weighted[...], side_high[...])
    gram = gram[0:S] + gram[S : 2 * S] + dot_nt(weighted[0:S, :], side_low[...])
    moments[432:480, :] = moments[432:480, :] - pltpu.roll(gram, 8, 1)
    moments[480:REGION, :] = jnp.zeros((REGION - 480, 128), F32)
    plane_start(moments, part_a, 0)

    for copy in halo:
        copy.wait_recv()
    first_row = row == 0
    last_row = row == ROWS - 1
    from_left = jnp.where(col == 0, 0.0, left_in[...])
    from_right = jnp.where(col == COLS - 1, 0.0, right_in[...])
    for t in range(16):
        c, s = divmod(t, 8)
        block = base[t]
        if s == 0:
            before = jnp.where(first_row, 0.0, up_in[c])
        else:
            before = base[t - 1]
        if s == 7:
            after = jnp.where(last_row, 0.0, down_in[c])
        else:
            after = base[t + 1]
        along = 0.5 * (after - before)
        ahead = jnp.where(lane56 == 127, pltpu.roll(from_right, 127 - t, 1), pltpu.roll(block, 127, 1))
        shifted = pltpu.roll(from_left, 128 - t, 1) if t else from_left
        behind = jnp.where(lane56 == 0, shifted, pltpu.roll(block, 1, 1))
        across = 0.5 * (ahead - behind)
        grad_x[t, 0:S, :] = along[0:S]
        grad_x[t, S : S + 24, :] = along[0:24]
        grad_x[t, 72:80, :] = along[S:56]
        grad_y[t, 0:S, :] = across[0:S]
        grad_y[t, S : S + 24, :] = across[0:24]
        grad_y[t, 72:80, :] = across[S:56]

    def pair_value(d, s, c, u0, u1, v0, v1):
        t = c * 8 + s
        ahead = pl.ds(d, S)
        return (
            u0 * grad_x[t, ahead, :] + u1 * grad_y[t, ahead, :]
            + v0 * grad_x[t, 0:S, :] + v1 * grad_y[t, 0:S, :]
        )

    def pair_block(d, carry):
        rows = pl.ds(pl.multiple_of(d * S, S), S)
        for s in range(8):
            u0, u1 = both[s, 0:S, :], both[8 + s, 0:S, :]
            v0, v1 = both[s, pl.ds(d, S), :], both[8 + s, pl.ds(d, S), :]
            for c in range(2):
                t = c * 8 + s
                high, low = split(pair_value(d, s, c, u0, u1, v0, v1))
                pair_high[rows, t * 128 : (t + 1) * 128] = high
                pair_low[rows, t * 128 : (t + 1) * 128] = low
        return carry

    for s in range(8):
        u0, u1 = both[s, 0:S, :], both[8 + s, 0:S, :]
        v0, v1 = both[s, 24:72, :], both[8 + s, 24:72, :]
        m0, m1 = base[s, S : S + 1, :], base[8 + s, S : S + 1, :]
        for c in range(2):
            t = c * 8 + s
            cells = slice(t * 128, (t + 1) * 128)
            value = u0 * grad_x[t, 0:S, :] + u1 * grad_y[t, 0:S, :]
            high, low = split(value)
            pair_high[0:S, cells] = high
            pair_low[0:S, cells] = low
            value = pair_value(24, s, c, u0, u1, v0, v1)
            minus = (
                m0 * grad_x[t, 0:S, :] + m1 * grad_y[t, 0:S, :]
                + u0 * grad_x[t, 72:73, :] + u1 * grad_y[t, 72:73, :]
            )
            back[t] = minus
            high, low = split(jnp.concatenate([value[0:24], minus[0:24]], axis=0))
            pair_high[1152:1200, cells] = high
            pair_low[1152:1200, cells] = low
            high, low = split(jnp.concatenate([minus[24:48], jnp.zeros((56, 128), F32)], axis=0))
            pair_high[1200:1280, cells] = high
            pair_low[1200:1280, cells] = low
    lax.fori_loop(1, 12, pair_block, 0)
    deep_start(moments, part_a, mine_a, deep_a, 0)
    lax.fori_loop(12, 24, pair_block, 0)
    gather_start(mine_a, deep_a, total_a, 0)

    def project(lb, carry):
        rows = pl.ds(pl.multiple_of(lb * 256, 256), 256)
        high = pair_high[rows, :]
        out = dot_nt(weighted[...], high)
        out = out[0:S] + out[S : 2 * S] + dot_nt(weighted[0:S, :], pair_low[rows, :])
        tensor[pl.ds(pl.multiple_of(lb * 96, 96), S), :] = out[:, 0:128]
        tensor[pl.ds(pl.multiple_of(lb * 96 + S, S), S), :] = out[:, 128:256]
        return carry

    lax.fori_loop(0, 5, project, 0)
    tensor[480:REGION, :] = jnp.zeros((REGION - 480, 128), F32)
    plane_start(tensor, part_b, 3)

    gather_wait(part_a, 0)
    tail = total_a[432:480, :]
    second = jnp.where(lane < S, pltpu.roll(tail, 128 - 24, 1), 0.0) * (1.0 / R)
    gram_inv[...] = jnp.where(lane < S, pltpu.roll(tail, 128 - 72, 1), 0.0)
    mean_col = jnp.sum(jnp.where(lane == 120, tail, 0.0), axis=1, keepdims=True) * (1.0 / R)
    mean_row = jnp.sum(jnp.where(lane == sub, mean_col, 0.0), axis=0, keepdims=True)
    cov_inv[...] = second - mean_col * mean_row
    for lb in range(10):
        number = lb * 128 + lane
        first_d = lb * 128 // S
        d = jnp.full((S, 128), first_d, jnp.int32)
        for step in range(first_d + 1, first_d + 4):
            d = d + jnp.where(number >= step * S, 1, 0)
        k = number - d * S
        l = k + d
        l = jnp.where(l >= S, l - S, l)
        hot_k = jnp.where(sub == k, 1.0, 0.0)
        hot_l = jnp.where(sub == l, 1.0, 0.0)
        at_k = exact(second, tall(hot_k))
        at_l = exact(second, tall(hot_l))
        mean_k = jnp.sum(mean_col * hot_k, axis=0, keepdims=True)
        mean_l = jnp.sum(mean_col * hot_l, axis=0, keepdims=True)
        second_kl = jnp.sum(hot_k * at_l, axis=0, keepdims=True)
        third = total_a[lb * S : (lb + 1) * S, :] * (1.0 / R)
        third = third - mean_col * (second_kl - 2.0 * (mean_k * mean_l)) - mean_k * at_l - mean_l * at_k
        cov = second_kl - mean_k * mean_l
        if lb == 9:
            third = jnp.where(lane < 24, third, 0.0)
            cov = jnp.where(lane1 < 24, cov, 0.0)
        cube[lb * S : (lb + 1) * S, :] = third
        high, low = split(third)
        cube_split[0:S, lb * 128 : (lb + 1) * 128] = high
        cube_split[S : 2 * S, lb * 128 : (lb + 1) * 128] = low
        pair_cov[lb : lb + 1, :] = cov

    def contract(n, carry):
        cells = pl.ds(pl.multiple_of(n * 256, 256), 256)
        out = dot(cube_split[...], pair_high[:, cells])
        out = out[0:S] + out[S : 2 * S] + dot(cube_split[0:S, :], pair_low[:, cells])
        high, low = split(out)
        side_high[0:S, cells] = high
        side_low[0:S, cells] = low
        return carry

    lax.fori_loop(0, 8, contract, 0)
    deep_start(tensor, part_b, mine_b, deep_b, 3)

    def eliminate(i, carry):
        for matrix in (cov_inv, gram_inv):
            value = matrix[...]
            line = matrix[pl.ds(i, 1), :]
            pivot = jnp.sum(jnp.where(lane1 == i, line, 0.0), axis=1, keepdims=True)
            column = jnp.sum(jnp.where(lane == i, value, 0.0), axis=1, keepdims=True)
            inverse = 1.0 / pivot
            line = jnp.where(lane1 == i, inverse, line * inverse)
            value = jnp.where(lane == i, 0.0, value) - column * line
            matrix[...] = jnp.where(sub == i, line, value)
        return carry

    lax.fori_loop(0, S, eliminate, 0)
    gather_start(mine_b, deep_b, total_b, 3)
    centred = raw - mean_col
    pair_up(centred, False)
    gather_wait(part_b, 3)

    cross = jnp.zeros((S, 128), F32)
    for lb in range(10):
        rows = slice(lb * S, (lb + 1) * S)
        cross = cross + exact_nt(total_b[rows, :], tall(cube[rows, :]))
    lin_proj = jnp.where(lane < S, pltpu.roll(total_b[432:480, :], 128 - 24, 1), 0.0)
    projected = lin_proj + exact(cross, tall(cov_inv[...]))
    solved = exact(gram_inv[...], tall(projected))
    unit = jnp.where(lane == sub, 1.0, 0.0)
    turned = exact_nt(unit, tall(solved))
    factors = jnp.where(lane < S, cov_inv[...], pltpu.roll(turned, 64, 1))
    high, low = split(factors)
    lowest = (factors - high.astype(F32) - low.astype(F32)).astype(BF16)
    factors = jnp.concatenate([high, low, lowest], axis=0)
    first_column = jnp.zeros((S, 128), F32)
    last_column = jnp.zeros((S, 128), F32)
    for n in range(8):
        cells = slice(n * 256, (n + 1) * 256)
        out = dot(factors, side_high[:, cells])
        rest = dot(factors[0 : 2 * S], side_low[:, cells])
        out = out[0:S] + out[S : 2 * S] + out[2 * S : 3 * S] + rest[0:S] + rest[S : 2 * S]
        for t in (2 * n, 2 * n + 1):
            c, s = divmod(t, 8)
            part = out[:, 0:128] if t % 2 == 0 else out[:, 128:256]
            mask = water[s : s + 1, :].astype(F32)
            value = mask * (both[t, 0:S, :] - STEP * (back[t] + part))
            half[t] = value
            shifted = pltpu.roll(value, t, 1) if t else value
            first_column = jnp.where(lane == t, shifted, first_column)
            last_column = jnp.where(lane == t, pltpu.roll(value, t + 1, 1), last_column)
            if s == 0:
                up_out2[c] = value
            if s == 7:
                down_out2[c] = value
    left_out2[...] = first_column
    right_out2[...] = last_column
    halo2 = copies(
        (up_out2, down_out2, left_out2, right_out2), (up_in2, down_in2, left_in2, right_in2), 4
    )
    for copy in halo2:
        copy.start()

    change = jnp.zeros((S, 128), F32)
    excess = jnp.zeros((S, 128), F32)
    for lb in range(10):
        here = total_b[lb * S : (lb + 1) * S, :]
        change = change + exact(here, pair_coeffs[lb * 128 : (lb + 1) * 128, :])
        excess = excess + here * pair_cov[lb : lb + 1, :]
    change = change - jnp.sum(excess, axis=1, keepdims=True)
    square[0:S, :] = centred + STEP * exact(gram_inv[...], tall(change))
    new_coeffs[...] = square[...].T[:, 0:S]

    for copy in halo2:
        copy.wait_recv()
    from_left = jnp.where(col == 0, 0.0, left_in2[...])
    from_right = jnp.where(col == COLS - 1, 0.0, right_in2[...])
    for t in range(16):
        c, s = divmod(t, 8)
        value = half[t]
        before = jnp.where(first_row, 0.0, up_in2[c]) if s == 0 else half[t - 1]
        after = jnp.where(last_row, 0.0, down_in2[c]) if s == 7 else half[t + 1]
        ahead = jnp.where(lane == 127, pltpu.roll(from_right, 127 - t, 1), pltpu.roll(value, 127, 1))
        shifted = pltpu.roll(from_left, 128 - t, 1) if t else from_left
        behind = jnp.where(lane == 0, shifted, pltpu.roll(value, 1, 1))
        laplace = after + before + ahead + behind - 4.0 * value
        mask = water[s : s + 1, :].astype(F32)
        new_modes[pl.ds(t, S, stride=16), :] = mask * (value + VISCOUS * laplace)

    for copy in halo + halo2:
        copy.wait_send()
    sums_sent(part_a, deep_a, 0)
    sums_sent(part_b, deep_b, 3)


def on_device(modes, mean_flow, seeds, amplitudes, water_mask):
    vmem = pl.BlockSpec(memory_space=pltpu.VMEM)

    def f32(*shape):
        return pltpu.VMEM(shape, F32)

    def bf16(*shape):
        return pltpu.VMEM(shape, BF16)

    sums = [
        f32((GROUP - 1) * CHUNK, 128), f32((DEEP - 1) * CHUNK, 128), f32(2 * CHUNK, 128), f32(REGION, 128)
    ]
    new_modes, new_coeffs = pl.pallas_call(
        kernel,
        out_shape=(
            jax.ShapeDtypeStruct((S * 16, 128), F32),
            jax.ShapeDtypeStruct((128, S), F32),
        ),
        in_specs=[vmem] * 5,
        out_specs=(vmem, vmem),
        scratch_shapes=[
            f32(16, 56, 128), f32(16, 72, 128), f32(16, 80, 128), f32(16, 80, 128), f32(16, S, 128),
            bf16(2 * S, 2048), bf16(WIDE, 2048), bf16(WIDE, 2048), bf16(128, 2048), bf16(128, 2048),
            f32(128, 128), f32(72, 128), f32(WIDE, 128),
            f32(REGION, 128), f32(REGION, 128), f32(480, 128), bf16(2 * S, WIDE),
            f32(16, 128), f32(S, 128), f32(S, 128), f32(16, S, 128),
            *sums, *sums,
            *([f32(2, 56, 128)] * 2 + [f32(56, 128)] * 2) * 2,
            *([f32(2, S, 128)] * 2 + [f32(S, 128)] * 2) * 2,
            pltpu.SemaphoreType.DMA((8,)), pltpu.SemaphoreType.DMA((8,)),
            pltpu.SemaphoreType.DMA((6,)), pltpu.SemaphoreType.DMA((6,)),
        ],
        compiler_params=pltpu.CompilerParams(
            collective_id=0, has_side_effects=True, vmem_limit_bytes=56 * 1024 * 1024
        ),
    )(
        modes.reshape(S * 16, 128),
        mean_flow.reshape(16, 128),
        seeds,
        amplitudes.reshape(1, S),
        water_mask,
    )
    return new_modes.reshape(S, 2, 8, 128), new_coeffs


def solution(mesh):
    return jax.shard_map(
        on_device,
        mesh=mesh,
        in_specs=(
            P(None, None, "row", "col"),
            P(None, "row", "col"),
            P(("row", "col"), None),
            P(),
            P("row", "col"),
        ),
        out_specs=(P(None, None, "row", "col"), P(("row", "col"), None)),
        check_vma=False,
    )
```

```python
import math

import jax
import jax.numpy as jnp
from jax import lax
from jax.experimental import pallas as pl
from jax.experimental.pallas import tpu as pltpu
from jax.sharding import PartitionSpec as P

F32 = jnp.float32
BF16 = jnp.bfloat16
MESH = pl.DeviceIdType.MESH
HIGHEST = lax.Precision.HIGHEST

S = 48
R = 32768
CELLS = 2.0 * 64 * 4096
STEP = 0.25
VISCOUS = 0.2
ROWS, COLS, ALONG_X = 8, 32, 4
GROUP = ROWS * ALONG_X
DEEP = COLS // ALONG_X
CHUNK = 16
REGION = GROUP * CHUNK
PAIRS = 1176
WIDE = 1280
INNER = [(c, s) for s in range(1, 7) for c in range(2)]
OUTER = [(c, s) for s in (0, 7) for c in range(2)]
SLOT = {place: number for number, place in enumerate(INNER + OUTER)}
SEAM = 16
LANES = 18 * 128
INNER_LANES = 12 * 128
NT = (((1,), (1,)), ((), ()))


def split(value):
    high = value.astype(BF16)
    return high, (value - high.astype(F32)).astype(BF16)


def dot(a, b):
    return jnp.dot(a, b, preferred_element_type=F32)


def dot_nt(a, b):
    return lax.dot_general(a, b, NT, preferred_element_type=F32)


def exact(a, b):
    return jnp.dot(a, b, precision=HIGHEST, preferred_element_type=F32)


def exact_nt(a, b):
    return lax.dot_general(a, b, NT, precision=HIGHEST, preferred_element_type=F32)


def tall(value):
    return jnp.concatenate([value, jnp.zeros((128 - S, 128), F32)], axis=0)


def kernel(
    modes_hbm, mean_hbm, seeds_hbm, amps_hbm, water_hbm, new_modes, new_coeffs,
    modes, mean, seeds, amps, water,
    base, both, grad_x, grad_y, back, weighted, pair_high, pair_low, side_high, side_low,
    seam_field, seam_slope, seam_back, amp_row, coeffs, pair_coeffs, moments, tensor, cube, cube_split, pair_cov,
    cov_inv, gram_inv, half, key_high, key_low,
    part_a, deep_a, mine_a, total_a, part_b, deep_b, mine_b, total_b,
    up_out, down_out, side_out, up_in, down_in, left_in, right_in,
    up_out2, down_out2, side_out2, up_in2, down_in2, left_in2, right_in2,
    halo_send, halo_recv, sum_send, sum_recv, fetch_sem,
):
    row = lax.axis_index("row")
    col = lax.axis_index("col")
    along_x = lax.rem(col, ALONG_X)
    plane = lax.div(col, ALONG_X)
    place = row * ALONG_X + along_x
    above = lax.rem(row + ROWS - 1, ROWS)
    below = lax.rem(row + 1, ROWS)
    left = lax.rem(col + COLS - 1, COLS)
    right = lax.rem(col + 1, COLS)

    def member(offset):
        other = lax.rem(place + offset, GROUP)
        return other, (lax.div(other, ALONG_X), plane * ALONG_X + lax.rem(other, ALONG_X))

    def deep(offset):
        return (row, lax.rem(plane + offset, DEEP) * ALONG_X + along_x)

    barrier = pltpu.get_barrier_semaphore()

    def greet_plane(offset, carry):
        pl.semaphore_signal(barrier, inc=1, device_id=member(offset)[1], device_id_type=MESH)
        return carry

    def greet_deep(offset, carry):
        pl.semaphore_signal(barrier, inc=1, device_id=deep(offset), device_id_type=MESH)
        return carry

    lax.fori_loop(1, GROUP, greet_plane, 0)
    lax.fori_loop(1, DEEP, greet_deep, 0)
    pl.semaphore_signal(barrier, inc=1, device_id=(row, left), device_id_type=MESH)
    pl.semaphore_signal(barrier, inc=1, device_id=(row, right), device_id_type=MESH)

    fetches = [
        pltpu.make_async_copy(source, target, fetch_sem.at[k])
        for k, (source, target) in enumerate(
            ((seeds_hbm, seeds), (amps_hbm, amps), (modes_hbm, modes), (mean_hbm, mean), (water_hbm, water))
        )
    ]
    for fetch in fetches:
        fetch.start()

    lane = lax.broadcasted_iota(jnp.int32, (S, 128), 1)
    lane1 = lax.broadcasted_iota(jnp.int32, (1, 128), 1)
    sub = lax.broadcasted_iota(jnp.int32, (S, 128), 0)
    sub8 = lax.broadcasted_iota(jnp.int32, (8, 128), 0)

    def copies(outs, ins, first):
        targets = ((above, col), (below, col), (row, left), (row, right))
        arrivals = (ins[1], ins[0], ins[3], ins[2])
        return [
            pltpu.make_async_remote_copy(
                src_ref=outs[k],
                dst_ref=arrivals[k],
                send_sem=halo_send.at[first + k],
                recv_sem=halo_recv.at[first + k],
                device_id=targets[k],
                device_id_type=MESH,
            )
            for k in range(4)
        ]

    def plane_start(source, parts, sems):
        def send(offset, carry):
            other, device = member(offset)
            pltpu.make_async_remote_copy(
                src_ref=source.at[pl.ds(pl.multiple_of(other * CHUNK, CHUNK), CHUNK)],
                dst_ref=parts.at[pl.ds(pl.multiple_of((offset - 1) * CHUNK, CHUNK), CHUNK)],
                send_sem=sum_send.at[sems],
                recv_sem=sum_recv.at[sems],
                device_id=device,
                device_id_type=MESH,
            ).start()
            return carry

        lax.fori_loop(1, GROUP, send, 0)

    def deep_start(source, parts, mine, deeper, sems):
        pltpu.make_async_copy(parts, parts, sum_recv.at[sems]).wait()
        value = source[pl.ds(pl.multiple_of(place * CHUNK, CHUNK), CHUNK), :]
        for k in range(GROUP - 1):
            value = value + parts[k * CHUNK : (k + 1) * CHUNK, :]
        mine[0:CHUNK, :] = value

        def send(offset, carry):
            pltpu.make_async_remote_copy(
                src_ref=mine.at[pl.ds(0, CHUNK)],
                dst_ref=deeper.at[pl.ds(pl.multiple_of((offset - 1) * CHUNK, CHUNK), CHUNK)],
                send_sem=sum_send.at[sems + 1],
                recv_sem=sum_recv.at[sems + 1],
                device_id=deep(offset),
                device_id_type=MESH,
            ).start()
            return carry

        lax.fori_loop(1, DEEP, send, 0)

    def gather_start(mine, deeper, total, sems):
        pltpu.make_async_copy(deeper, deeper, sum_recv.at[sems + 1]).wait()
        value = mine[0:CHUNK, :]
        for k in range(DEEP - 1):
            value = value + deeper[k * CHUNK : (k + 1) * CHUNK, :]
        mine[CHUNK : 2 * CHUNK, :] = value
        own = pl.ds(pl.multiple_of(place * CHUNK, CHUNK), CHUNK)
        total[own, :] = value

        def send(offset, carry):
            pltpu.make_async_remote_copy(
                src_ref=mine.at[pl.ds(CHUNK, CHUNK)],
                dst_ref=total.at[own],
                send_sem=sum_send.at[sems + 2],
                recv_sem=sum_recv.at[sems + 2],
                device_id=member(offset)[1],
                device_id_type=MESH,
            ).start()
            return carry

        lax.fori_loop(1, GROUP, send, 0)

    def gather_wait(parts, sems):
        pltpu.make_async_copy(parts, parts, sum_recv.at[sems + 2]).wait()

    def sums_sent(parts, deeper, sems):
        pltpu.make_async_copy(parts, parts, sum_send.at[sems]).wait()
        pltpu.make_async_copy(deeper, deeper, sum_send.at[sems + 1]).wait()
        pltpu.make_async_copy(parts, parts, sum_send.at[sems + 2]).wait()

    for fetch in fetches[:2]:
        fetch.wait()
    phase = seeds[...].astype(F32) * (3.0 * math.pi / 8192.0)
    wave = jnp.cos(phase)
    strength = 0.5 + ((row * COLS + col) * 128 + lane).astype(F32) * (1.0 / R)
    amp_row[...] = jnp.zeros((8, 128), F32)
    amp_row[0:1, 0:S] = amps[...]
    amp_col = jnp.sum(jnp.where(lane == sub, amp_row[0:1, :], 0.0), axis=1, keepdims=True)
    raw = strength * amp_col * (wave + (wave * wave - 0.5))

    def pair_up(values, ones):
        coeffs[0:S, :] = values
        coeffs[S : S + 24, :] = values[0:24]
        for d in range(24):
            pair_coeffs[d * S : (d + 1) * S, :] = values * coeffs[d : d + S, :]
        pair_coeffs[1152:PAIRS, :] = values[0:24] * coeffs[24:48, :]
        pair_coeffs[PAIRS : PAIRS + S, :] = values
        pair_coeffs[PAIRS + S : WIDE, :] = jnp.zeros((WIDE - PAIRS - S, 128), F32)
        if ones:
            pair_coeffs[1272:1280, :] = jnp.where(sub8 == 0, 1.0, 0.0)

    pair_up(raw, True)
    for lb in range(5):
        out = exact_nt(raw, pair_coeffs[lb * 256 : (lb + 1) * 256, :])
        moments[lb * 96 : lb * 96 + S, :] = out[:, 0:128]
        moments[lb * 96 + S : lb * 96 + 96, :] = out[:, 128:256]
    for fetch in fetches[2:]:
        fetch.wait()

    def lanes_of(c, s):
        return slice(SLOT[c, s] * 128, (SLOT[c, s] + 1) * 128)

    seam_lanes = slice(SEAM * 128, LANES)
    side_high[...] = jnp.zeros((128, LANES), BF16)
    side_low[...] = jnp.zeros((128, LANES), BF16)
    lane56 = lax.broadcasted_iota(jnp.int32, (56, 128), 1)
    columns = jnp.zeros((56, 128), F32)
    shore = jnp.zeros((1, 128), F32)
    for t in range(16):
        c, s = divmod(t, 8)
        field = modes[pl.ds(t, S, stride=16), :]
        drift_row = jnp.where(sub8 == 0, jnp.broadcast_to(mean[t : t + 1, :], (8, 128)), 0.0)
        block = jnp.concatenate([field, drift_row], axis=0)
        base[t] = block
        both[t, 0:S, :] = field
        both[t, S : S + 24, :] = field[0:24]
        weight = water[s : s + 1, :].astype(F32) * (-1.0 / CELLS)
        high, low = split(field * weight)
        weighted[0:S, lanes_of(c, s)] = high
        weighted[S : 2 * S, lanes_of(c, s)] = low
        high, low = split(field)
        side_high[64 : 64 + S, lanes_of(c, s)] = high
        side_low[64 : 64 + S, lanes_of(c, s)] = low
        columns = jnp.where(lane56 == 64 + t, pltpu.roll(block, 64 + t, 1), columns)
        columns = jnp.where(lane56 == t, pltpu.roll(block, t + 1, 1), columns)
        shore = jnp.where(lane1 == t, pltpu.roll(weight, t, 1) if t else weight, shore)
        shore = jnp.where(lane1 == 64 + t, pltpu.roll(weight, 65 + t, 1), shore)
        if s == 0:
            up_out[c] = block
        if s == 7:
            down_out[c] = block
        ahead = jnp.where(lane56 == 127, 0.0, pltpu.roll(block, 127, 1))
        behind = jnp.where(lane56 == 0, 0.0, pltpu.roll(block, 1, 1))
        across = 0.5 * (ahead - behind)
        grad_y[t, 0:S, :] = across[0:S]
        grad_y[t, S : S + 24, :] = across[0:24]
        grad_y[t, 72:80, :] = across[S:56]
    side_out[...] = columns

    def slope(t, before, after):
        along = 0.5 * (after - before)
        grad_x[t, 0:S, :] = along[0:S]
        grad_x[t, S : S + 24, :] = along[0:24]
        grad_x[t, 72:80, :] = along[S:56]

    for c, s in INNER:
        slope(c * 8 + s, base[c * 8 + s - 1], base[c * 8 + s + 1])

    own = pltpu.roll(columns, 64, 1)
    high, low = split(own[0:S] * shore)
    weighted[0:S, seam_lanes] = jnp.concatenate([high, jnp.zeros((S, 128), BF16)], axis=1)
    weighted[S : 2 * S, seam_lanes] = jnp.concatenate([low, jnp.zeros((S, 128), BF16)], axis=1)
    second_half = lax.rem(lax.div(lane56, 8), 2) == 1
    own = jnp.where(second_half, own, pltpu.roll(own, 120, 1))
    seam_field[0:S, :] = own[0:S]
    seam_field[S : S + 24, :] = own[0:24]
    seam_field[72:80, :] = own[S:56]

    gram = dot_nt(weighted[...], side_high[...])
    gram = gram[0:S] + gram[S : 2 * S] + dot_nt(weighted[0:S, :], side_low[...])
    moments[432:480, :] = moments[432:480, :] - pltpu.roll(gram, 8, 1)
    moments[480:REGION, :] = jnp.zeros((REGION - 480, 128), F32)
    pl.semaphore_wait(barrier, GROUP - 1 + DEEP - 1 + 2)
    halo = copies(
        (up_out, down_out, side_out, side_out), (up_in, down_in, left_in, right_in), 0
    )
    for copy in halo:
        copy.start()
    plane_start(moments, part_a, 0)

    def pair_value(d, t, u0, u1, v0, v1):
        ahead = pl.ds(d, S)
        return (
            u0 * grad_x[t, ahead, :] + u1 * grad_y[t, ahead, :]
            + v0 * grad_x[t, 0:S, :] + v1 * grad_y[t, 0:S, :]
        )

    def store(rows, lanes, value):
        high, low = split(value)
        pair_high[rows, lanes] = high
        pair_low[rows, lanes] = low

    def pairs_of(grid_rows):
        def pair_block(d, carry):
            rows = pl.ds(pl.multiple_of(d * S, S), S)
            for s in grid_rows:
                u0, u1 = both[s, 0:S, :], both[8 + s, 0:S, :]
                v0, v1 = both[s, pl.ds(d, S), :], both[8 + s, pl.ds(d, S), :]
                for c in range(2):
                    store(rows, lanes_of(c, s), pair_value(d, c * 8 + s, u0, u1, v0, v1))
            return carry

        return pair_block

    def last_rows(lanes, value, minus):
        store(slice(1152, 1200), lanes, jnp.concatenate([value[0:24], minus[0:24]], axis=0))
        store(slice(1200, WIDE), lanes, jnp.concatenate([minus[24:48], jnp.zeros((56, 128), F32)], axis=0))

    def other_pairs(grid_rows):
        for s in grid_rows:
            u0, u1 = both[s, 0:S, :], both[8 + s, 0:S, :]
            v0, v1 = both[s, 24:72, :], both[8 + s, 24:72, :]
            m0, m1 = base[s, S : S + 1, :], base[8 + s, S : S + 1, :]
            for c in range(2):
                t = c * 8 + s
                store(slice(0, S), lanes_of(c, s), u0 * grad_x[t, 0:S, :] + u1 * grad_y[t, 0:S, :])
                minus = (
                    m0 * grad_x[t, 0:S, :] + m1 * grad_y[t, 0:S, :]
                    + u0 * grad_x[t, 72:73, :] + u1 * grad_y[t, 72:73, :]
                )
                back[t] = minus
                last_rows(lanes_of(c, s), pair_value(24, t, u0, u1, v0, v1), minus)

    def project_of(lanes, add):
        def project(lb, carry):
            rows = pl.ds(pl.multiple_of(lb * 256, 256), 256)
            out = dot_nt(weighted[:, lanes], pair_high[rows, lanes])
            out = out[0:S] + out[S : 2 * S] + dot_nt(weighted[0:S, lanes], pair_low[rows, lanes])
            for k in range(2):
                to = pl.ds(pl.multiple_of(lb * 96 + k * S, S), S)
                part = out[:, k * 128 : (k + 1) * 128]
                tensor[to, :] = tensor[to, :] + part if add else part
            return carry

        return project

    other_pairs(range(1, 7))
    lax.fori_loop(1, 24, pairs_of(range(1, 7)), 0)
    lax.fori_loop(0, 5, project_of(slice(0, INNER_LANES), False), 0)

    for copy in halo:
        copy.wait_recv()
    for c in range(2):
        slope(c * 8, jnp.where(row == 0, 0.0, up_in[c]), base[c * 8 + 1])
        slope(c * 8 + 7, base[c * 8 + 6], jnp.where(row == ROWS - 1, 0.0, down_in[c]))
    from_left = jnp.where(col == 0, 0.0, left_in[...])
    from_right = jnp.where(col == COLS - 1, 0.0, right_in[...])
    change = jnp.where(lane56 < 64, -0.5 * from_left, 0.5 * from_right)
    seam_slope[0:S, :] = change[0:S]
    seam_slope[S : S + 24, :] = change[0:24]
    seam_slope[72:80, :] = change[S:56]
    seam = slice(SEAM * 128, (SEAM + 1) * 128)

    def seam_value(d):
        ahead = pl.ds(d, S)
        return seam_field[0:S, :] * seam_slope[ahead, :] + seam_field[ahead, :] * seam_slope[0:S, :]

    def seam_pairs(d, carry):
        store(pl.ds(pl.multiple_of(d * S, S), S), seam, seam_value(d))
        return pairs_of((0, 7))(d, carry)

    other_pairs((0, 7))
    minus = seam_field[72:73, :] * seam_slope[0:S, :] + seam_field[0:S, :] * seam_slope[72:73, :]
    seam_back[...] = minus
    store(slice(0, S), seam, seam_field[0:S, :] * seam_slope[0:S, :])
    last_rows(seam, seam_value(24), minus)
    pair_high[:, 17 * 128 : LANES] = jnp.zeros((WIDE, 128), BF16)
    pair_low[:, 17 * 128 : LANES] = jnp.zeros((WIDE, 128), BF16)
    lax.fori_loop(1, 24, seam_pairs, 0)

    lax.fori_loop(0, 5, project_of(slice(INNER_LANES, LANES), True), 0)
    tensor[480:REGION, :] = jnp.zeros((REGION - 480, 128), F32)
    plane_start(tensor, part_b, 3)
    deep_start(moments, part_a, mine_a, deep_a, 0)
    gather_start(mine_a, deep_a, total_a, 0)
    deep_start(tensor, part_b, mine_b, deep_b, 3)

    gather_start(mine_b, deep_b, total_b, 3)
    gather_wait(part_a, 0)
    tail = total_a[432:480, :]
    second = jnp.where(lane < S, pltpu.roll(tail, 128 - 24, 1), 0.0) * (1.0 / R)
    gram_inv[...] = jnp.where(lane < S, pltpu.roll(tail, 128 - 72, 1), 0.0)
    mean_col = jnp.sum(jnp.where(lane == 120, tail, 0.0), axis=1, keepdims=True) * (1.0 / R)
    mean_row = jnp.sum(jnp.where(lane == sub, mean_col, 0.0), axis=0, keepdims=True)
    cov_inv[...] = second - mean_col * mean_row
    for lb in range(10):
        number = lb * 128 + lane
        first_d = lb * 128 // S
        d = jnp.full((S, 128), first_d, jnp.int32)
        for step in range(first_d + 1, first_d + 4):
            d = d + jnp.where(number >= step * S, 1, 0)
        k = number - d * S
        l = k + d
        l = jnp.where(l >= S, l - S, l)
        hot_k = jnp.where(sub == k, 1.0, 0.0)
        hot_l = jnp.where(sub == l, 1.0, 0.0)
        at_k = exact(second, tall(hot_k))
        at_l = exact(second, tall(hot_l))
        mean_k = jnp.sum(mean_col * hot_k, axis=0, keepdims=True)
        mean_l = jnp.sum(mean_col * hot_l, axis=0, keepdims=True)
        second_kl = jnp.sum(hot_k * at_l, axis=0, keepdims=True)
        third = total_a[lb * S : (lb + 1) * S, :] * (1.0 / R)
        third = third - mean_col * (second_kl - 2.0 * (mean_k * mean_l)) - mean_k * at_l - mean_l * at_k
        cov = second_kl - mean_k * mean_l
        if lb == 9:
            third = jnp.where(lane < 24, third, 0.0)
            cov = jnp.where(lane1 < 24, cov, 0.0)
        cube[lb * S : (lb + 1) * S, :] = third
        high, low = split(third)
        cube_split[0:S, lb * 128 : (lb + 1) * 128] = high
        cube_split[S : 2 * S, lb * 128 : (lb + 1) * 128] = low
        pair_cov[lb : lb + 1, :] = cov

    def contract(n, carry):
        cells = pl.ds(pl.multiple_of(n * 256, 256), 256)
        out = dot(cube_split[...], pair_high[:, cells])
        out = out[0:S] + out[S : 2 * S] + dot(cube_split[0:S, :], pair_low[:, cells])
        high, low = split(out)
        side_high[0:S, cells] = high
        side_low[0:S, cells] = low
        return carry

    def picked(at, values, axis):
        return jnp.sum(jnp.where(at, values, 0.0), axis=axis, keepdims=True)

    def eliminate(i, carry):
        p = 2 * i
        for matrix in (cov_inv, gram_inv):
            value = matrix[...]
            line_p, line_q = matrix[pl.ds(p, 1), :], matrix[pl.ds(p + 1, 1), :]
            at_p, at_q = lane1 == p, lane1 == p + 1
            a, b, d = picked(at_p, line_p, 1), picked(at_q, line_p, 1), picked(at_q, line_q, 1)
            column_p, column_q = picked(lane == p, value, 1), picked(lane == p + 1, value, 1)
            inverse = 1.0 / a
            ratio = b * inverse
            g = 1.0 / (d - b * ratio)
            f = -ratio * g
            e = inverse - ratio * f
            new_p = jnp.where(at_p, e, jnp.where(at_q, f, e * line_p + f * line_q))
            new_q = jnp.where(at_p, f, jnp.where(at_q, g, f * line_p + g * line_q))
            value = jnp.where((lane == p) | (lane == p + 1), 0.0, value)
            value = value - column_p * new_p - column_q * new_q
            matrix[...] = jnp.where(sub == p, new_p, jnp.where(sub == p + 1, new_q, value))
        return carry

    def contract_and_eliminate(n, carry):
        contract(n, carry)
        for k in range(3):
            eliminate(n * 3 + k, carry)
        return carry

    lax.fori_loop(0, 8, contract_and_eliminate, 0)
    contract(8, 0)

    for lb in range(10):
        value = exact(cov_inv[...], tall(cube[lb * S : (lb + 1) * S, :]))
        if lb == 9:
            value = jnp.where(lane == sub + 24, 1.0, value)
        high, low = split(value)
        key_high[0:S, lb * 128 : (lb + 1) * 128] = high
        key_low[0:S, lb * 128 : (lb + 1) * 128] = low
    key_high[S:128, :] = jnp.zeros((128 - S, WIDE), BF16)
    key_low[S:128, :] = jnp.zeros((128 - S, WIDE), BF16)

    def split3(value):
        high, low = split(value)
        lowest = (value - high.astype(F32) - low.astype(F32)).astype(BF16)
        return jnp.concatenate([high, low, lowest], axis=0)

    def product(factors, cells):
        out = dot(factors, side_high[:, cells])
        rest = dot(factors[0 : 2 * S], side_low[:, cells])
        return out[0:S] + out[S : 2 * S] + out[2 * S : 3 * S] + rest[0:S] + rest[S : 2 * S]

    from_cov = split3(cov_inv[...])
    from_gram = split3(pltpu.roll(gram_inv[...], 64, 1))
    seam_part = product(from_cov, slice(2048, LANES))[:, 0:128] + seam_back[...]
    for n in range(8):
        cells = slice(n * 256, (n + 1) * 256)
        out = product(from_cov, cells)
        high, low = split(product(from_gram, cells))
        side_high[64 : 64 + S, cells] = high
        side_low[64 : 64 + S, cells] = low
        for k in range(2):
            c, s = (INNER + OUTER)[2 * n + k]
            t = c * 8 + s
            part = back[t] + out[:, k * 128 : (k + 1) * 128]
            at_left = pltpu.roll(seam_part, 128 - t, 1) if t else seam_part
            part = part + jnp.where(lane == 0, at_left, 0.0)
            part = part + jnp.where(lane == 127, pltpu.roll(seam_part, 63 - t, 1), 0.0)
            half[t] = both[t, 0:S, :] - STEP * part
    centred = raw - mean_col
    pair_up(centred, False)
    gather_wait(part_b, 3)

    totals = split3(jnp.concatenate([total_b[lb * S : (lb + 1) * S, :] for lb in range(10)], axis=1))
    out = dot_nt(totals, key_high[...])
    rest = dot_nt(totals[0 : 2 * S], key_low[...])
    out = out[0:S] + out[S : 2 * S] + out[2 * S : 3 * S] + rest[0:S] + rest[S : 2 * S]
    from_sums = split3(pltpu.roll(tall(out).T[0:S], 64, 1))
    columns = jnp.zeros((S, 128), F32)
    for n in range(8):
        out = product(from_sums, slice(n * 256, (n + 1) * 256))
        for k in range(2):
            c, s = (INNER + OUTER)[2 * n + k]
            t = c * 8 + s
            value = half[t] - STEP * out[:, k * 128 : (k + 1) * 128]
            value = water[s : s + 1, :].astype(F32) * value
            half[t] = value
            columns = jnp.where(lane == 64 + t, pltpu.roll(value, 64 + t, 1), columns)
            columns = jnp.where(lane == t, pltpu.roll(value, t + 1, 1), columns)
            if s == 0:
                up_out2[c] = value
            if s == 7:
                down_out2[c] = value
    side_out2[...] = columns
    halo2 = copies(
        (up_out2, down_out2, side_out2, side_out2), (up_in2, down_in2, left_in2, right_in2), 4
    )
    for copy in halo2:
        copy.start()

    change = jnp.zeros((S, 128), F32)
    excess = jnp.zeros((S, 128), F32)
    for lb in range(10):
        here = total_b[lb * S : (lb + 1) * S, :]
        change = change + exact(here, pair_coeffs[lb * 128 : (lb + 1) * 128, :])
        excess = excess + here * pair_cov[lb : lb + 1, :]
    change = change - jnp.sum(excess, axis=1, keepdims=True)
    new_coeffs[...] = centred + STEP * exact(gram_inv[...], tall(change))

    for copy in halo2:
        copy.wait_recv()
    from_left = jnp.where(col == 0, 0.0, left_in2[...])
    from_right = jnp.where(col == COLS - 1, 0.0, right_in2[...])
    for t in range(16):
        c, s = divmod(t, 8)
        value = half[t]
        before = jnp.where(row == 0, 0.0, up_in2[c]) if s == 0 else half[t - 1]
        after = jnp.where(row == ROWS - 1, 0.0, down_in2[c]) if s == 7 else half[t + 1]
        ahead = jnp.where(lane == 127, pltpu.roll(from_right, 63 - t, 1), pltpu.roll(value, 127, 1))
        shifted = pltpu.roll(from_left, 128 - t, 1) if t else from_left
        behind = jnp.where(lane == 0, shifted, pltpu.roll(value, 1, 1))
        laplace = after + before + ahead + behind - 4.0 * value
        mask = water[s : s + 1, :].astype(F32)
        new_modes[pl.ds(t, S, stride=16), :] = mask * (value + VISCOUS * laplace)

    for copy in halo + halo2:
        copy.wait_send()
    sums_sent(part_a, deep_a, 0)
    sums_sent(part_b, deep_b, 3)


def on_device(modes, mean_flow, seeds, amplitudes, water_mask):
    vmem = pl.BlockSpec(memory_space=pltpu.VMEM)

    def f32(*shape):
        return pltpu.VMEM(shape, F32)

    def bf16(*shape):
        return pltpu.VMEM(shape, BF16)

    sums = [
        f32((GROUP - 1) * CHUNK, 128), f32((DEEP - 1) * CHUNK, 128), f32(2 * CHUNK, 128), f32(REGION, 128)
    ]
    new_modes, new_coeffs = pl.pallas_call(
        kernel,
        out_shape=(
            jax.ShapeDtypeStruct((S * 16, 128), F32),
            jax.ShapeDtypeStruct((S, 128), F32),
        ),
        in_specs=[pl.BlockSpec(memory_space=pltpu.MemorySpace.HBM)] * 5,
        out_specs=(vmem, vmem),
        scratch_shapes=[
            f32(S * 16, 128), f32(16, 128), pltpu.VMEM((S, 128), jnp.int32), f32(1, S), pltpu.VMEM((8, 128), jnp.int32),
            f32(16, 56, 128), f32(16, 72, 128), f32(16, 80, 128), f32(16, 80, 128), f32(16, S, 128),
            bf16(2 * S, LANES), bf16(WIDE, LANES), bf16(WIDE, LANES), bf16(128, LANES), bf16(128, LANES),
            f32(80, 128), f32(80, 128), f32(S, 128), f32(8, 128), f32(72, 128), f32(WIDE, 128),
            f32(REGION, 128), f32(REGION, 128), f32(480, 128), bf16(2 * S, WIDE),
            f32(16, 128), f32(S, 128), f32(S, 128), f32(16, S, 128), bf16(128, WIDE), bf16(128, WIDE),
            *sums, *sums,
            f32(2, 56, 128), f32(2, 56, 128), f32(56, 128), f32(2, 56, 128), f32(2, 56, 128), f32(56, 128), f32(56, 128),
            f32(2, S, 128), f32(2, S, 128), f32(S, 128), f32(2, S, 128), f32(2, S, 128), f32(S, 128), f32(S, 128),
            pltpu.SemaphoreType.DMA((8,)), pltpu.SemaphoreType.DMA((8,)),
            pltpu.SemaphoreType.DMA((6,)), pltpu.SemaphoreType.DMA((6,)), pltpu.SemaphoreType.DMA((5,)),
        ],
        compiler_params=pltpu.CompilerParams(
            collective_id=0, has_side_effects=True, vmem_limit_bytes=32 * 1024 * 1024
        ),
    )(
        *(
            pltpu.with_memory_space_constraint(value, pltpu.MemorySpace.HBM)
            for value in (
                modes.reshape(S * 16, 128),
                mean_flow.reshape(16, 128),
                seeds.T,
                amplitudes.reshape(1, S),
                water_mask,
            )
        )
    )
    return new_modes.reshape(S, 2, 8, 128), new_coeffs.T


def solution(mesh):
    return jax.shard_map(
        on_device,
        mesh=mesh,
        in_specs=(
            P(None, None, "row", "col"),
            P(None, "row", "col"),
            P(("row", "col"), None),
            P(),
            P("row", "col"),
        ),
        out_specs=(P(None, None, "row", "col"), P(("row", "col"), None)),
        check_vma=False,
    )
```

```python
import math

import jax
import jax.numpy as jnp
from jax import lax
from jax.experimental import pallas as pl
from jax.experimental.pallas import tpu as pltpu
from jax.sharding import PartitionSpec as P

F32 = jnp.float32
BF16 = jnp.bfloat16
MESH = pl.DeviceIdType.MESH
HIGHEST = lax.Precision.HIGHEST

S = 48
R = 32768
CELLS = 2.0 * 64 * 4096
STEP = 0.25
VISCOUS = 0.2
ROWS, COLS, ALONG_X = 8, 32, 4
GROUP = ROWS * ALONG_X
DEEP = COLS // ALONG_X
CHUNK = 16
REGION = GROUP * CHUNK
HALF_CHUNK = CHUNK // 2
HALF_REGION = GROUP * HALF_CHUNK
PAIRS = 1176
WIDE = 1280
INNER = [(c, s) for s in range(1, 7) for c in range(2)]
OUTER = [(c, s) for s in (0, 7) for c in range(2)]
SLOT = {place: number for number, place in enumerate(INNER + OUTER)}
SEAM = 16
LANES = 18 * 128
NT = (((1,), (1,)), ((), ()))


def split(value):
    high = value.astype(BF16)
    return high, (value - high.astype(F32)).astype(BF16)


def dot(a, b):
    return jnp.dot(a, b, preferred_element_type=F32)


def dot_nt(a, b):
    return lax.dot_general(a, b, NT, preferred_element_type=F32)


def exact(a, b):
    return jnp.dot(a, b, precision=HIGHEST, preferred_element_type=F32)


def exact_nt(a, b):
    return lax.dot_general(a, b, NT, precision=HIGHEST, preferred_element_type=F32)


def tall(value):
    return jnp.concatenate([value, jnp.zeros((128 - S, 128), F32)], axis=0)


def kernel(
    modes_hbm, mean_hbm, seeds_hbm, amps_hbm, water_hbm, new_modes, new_coeffs,
    modes, mean, seeds, amps, water,
    base, both, grad_x, grad_y, back, weighted, pair_high, pair_low, side_high, side_low,
    seam_field, seam_slope, seam_back, amp_row, coeffs, pair_coeffs, moments, tensor_b, tensor_c, cube, cube_split, pair_cov,
    cov_inv, gram_inv, half, key_high, key_low,
    part_a, deep_a, mine_a, total_a, part_b, deep_b, mine_b, total_b, part_c, deep_c, mine_c, total_c,
    up_out, down_out, side_out, up_in, down_in, left_in, right_in,
    up_out2, down_out2, side_out2, up_in2, down_in2, left_in2, right_in2,
    halo_send, halo_recv, sum_send, sum_recv, fetch_sem,
):
    row = lax.axis_index("row")
    col = lax.axis_index("col")
    along_x = lax.rem(col, ALONG_X)
    plane = lax.div(col, ALONG_X)
    place = row * ALONG_X + along_x
    above = lax.rem(row + ROWS - 1, ROWS)
    below = lax.rem(row + 1, ROWS)
    left = lax.rem(col + COLS - 1, COLS)
    right = lax.rem(col + 1, COLS)

    def member(offset):
        other = lax.rem(place + offset, GROUP)
        return other, (lax.div(other, ALONG_X), plane * ALONG_X + lax.rem(other, ALONG_X))

    def deep(offset):
        return (row, lax.rem(plane + offset, DEEP) * ALONG_X + along_x)

    barrier = pltpu.get_barrier_semaphore()

    def greet_plane(offset, carry):
        pl.semaphore_signal(barrier, inc=1, device_id=member(offset)[1], device_id_type=MESH)
        return carry

    def greet_deep(offset, carry):
        pl.semaphore_signal(barrier, inc=1, device_id=deep(offset), device_id_type=MESH)
        return carry

    for offset in range(1, GROUP):
        greet_plane(offset, 0)
    for offset in range(1, DEEP):
        greet_deep(offset, 0)
    pl.semaphore_signal(barrier, inc=1, device_id=(row, left), device_id_type=MESH)
    pl.semaphore_signal(barrier, inc=1, device_id=(row, right), device_id_type=MESH)

    fetches = [
        pltpu.make_async_copy(source, target, fetch_sem.at[k])
        for k, (source, target) in enumerate(
            ((seeds_hbm, seeds), (amps_hbm, amps), (modes_hbm, modes), (mean_hbm, mean), (water_hbm, water))
        )
    ]
    for fetch in fetches:
        fetch.start()

    lane = lax.broadcasted_iota(jnp.int32, (S, 128), 1)
    lane1 = lax.broadcasted_iota(jnp.int32, (1, 128), 1)
    sub = lax.broadcasted_iota(jnp.int32, (S, 128), 0)
    sub8 = lax.broadcasted_iota(jnp.int32, (8, 128), 0)

    def copies(outs, ins, first):
        targets = ((above, col), (below, col), (row, left), (row, right))
        arrivals = (ins[1], ins[0], ins[3], ins[2])
        return [
            pltpu.make_async_remote_copy(
                src_ref=outs[k],
                dst_ref=arrivals[k],
                send_sem=halo_send.at[first + k],
                recv_sem=halo_recv.at[first + k],
                device_id=targets[k],
                device_id_type=MESH,
            )
            for k in range(4)
        ]

    def plane_start(source, parts, sems, chunk):
        def send(offset, carry):
            other, device = member(offset)
            pltpu.make_async_remote_copy(
                src_ref=source.at[pl.ds(pl.multiple_of(other * chunk, chunk), chunk)],
                dst_ref=parts.at[pl.ds(pl.multiple_of((offset - 1) * chunk, chunk), chunk)],
                send_sem=sum_send.at[sems],
                recv_sem=sum_recv.at[sems],
                device_id=device,
                device_id_type=MESH,
            ).start()
            return carry

        for offset in range(1, GROUP):
            send(offset, 0)

    def deep_start(source, parts, mine, deeper, sems, chunk):
        pltpu.make_async_copy(parts, parts, sum_recv.at[sems]).wait()
        value = source[pl.ds(pl.multiple_of(place * chunk, chunk), chunk), :]
        for k in range(GROUP - 1):
            value = value + parts[k * chunk : (k + 1) * chunk, :]
        mine[0:chunk, :] = value

        def send(offset, carry):
            pltpu.make_async_remote_copy(
                src_ref=mine.at[pl.ds(0, chunk)],
                dst_ref=deeper.at[pl.ds(pl.multiple_of((offset - 1) * chunk, chunk), chunk)],
                send_sem=sum_send.at[sems + 1],
                recv_sem=sum_recv.at[sems + 1],
                device_id=deep(offset),
                device_id_type=MESH,
            ).start()
            return carry

        for offset in range(1, DEEP):
            send(offset, 0)

    def gather_start(mine, deeper, total, sems, chunk):
        pltpu.make_async_copy(deeper, deeper, sum_recv.at[sems + 1]).wait()
        value = mine[0:chunk, :]
        for k in range(DEEP - 1):
            value = value + deeper[k * chunk : (k + 1) * chunk, :]
        mine[chunk : 2 * chunk, :] = value
        own = pl.ds(pl.multiple_of(place * chunk, chunk), chunk)
        total[own, :] = value

        def send(offset, carry):
            pltpu.make_async_remote_copy(
                src_ref=mine.at[pl.ds(chunk, chunk)],
                dst_ref=total.at[own],
                send_sem=sum_send.at[sems + 2],
                recv_sem=sum_recv.at[sems + 2],
                device_id=member(offset)[1],
                device_id_type=MESH,
            ).start()
            return carry

        for offset in range(1, GROUP):
            send(offset, 0)

    def gather_wait(parts, sems):
        pltpu.make_async_copy(parts, parts, sum_recv.at[sems + 2]).wait()

    def sums_sent(parts, deeper, sems):
        pltpu.make_async_copy(parts, parts, sum_send.at[sems]).wait()
        pltpu.make_async_copy(deeper, deeper, sum_send.at[sems + 1]).wait()
        pltpu.make_async_copy(parts, parts, sum_send.at[sems + 2]).wait()

    for fetch in fetches[:2]:
        fetch.wait()
    phase = seeds[...].astype(F32) * (3.0 * math.pi / 8192.0)
    wave = jnp.cos(phase)
    strength = 0.5 + ((row * COLS + col) * 128 + lane).astype(F32) * (1.0 / R)
    amp_row[...] = jnp.zeros((8, 128), F32)
    amp_row[0:1, 0:S] = amps[...]
    amp_col = jnp.sum(jnp.where(lane == sub, amp_row[0:1, :], 0.0), axis=1, keepdims=True)
    raw = strength * amp_col * (wave + (wave * wave - 0.5))

    def pair_up(values, ones):
        coeffs[0:S, :] = values
        coeffs[S : S + 24, :] = values[0:24]
        for d in range(24):
            pair_coeffs[d * S : (d + 1) * S, :] = values * coeffs[d : d + S, :]
        pair_coeffs[1152:PAIRS, :] = values[0:24] * coeffs[24:48, :]
        pair_coeffs[PAIRS : PAIRS + S, :] = values
        pair_coeffs[PAIRS + S : WIDE, :] = jnp.zeros((WIDE - PAIRS - S, 128), F32)
        if ones:
            pair_coeffs[1272:1280, :] = jnp.where(sub8 == 0, 1.0, 0.0)

    pair_up(raw, True)
    for lb in range(5):
        out = exact_nt(raw, pair_coeffs[lb * 256 : (lb + 1) * 256, :])
        moments[lb * 96 : lb * 96 + S, :] = out[:, 0:128]
        moments[lb * 96 + S : lb * 96 + 96, :] = out[:, 128:256]
    for fetch in fetches[2:]:
        fetch.wait()

    def lanes_of(c, s):
        return slice(SLOT[c, s] * 128, (SLOT[c, s] + 1) * 128)

    seam_lanes = slice(SEAM * 128, LANES)
    side_high[...] = jnp.zeros((128, LANES), BF16)
    side_low[...] = jnp.zeros((128, LANES), BF16)
    lane56 = lax.broadcasted_iota(jnp.int32, (56, 128), 1)
    columns = jnp.zeros((56, 128), F32)
    shore = jnp.zeros((1, 128), F32)
    for t in range(16):
        c, s = divmod(t, 8)
        field = modes[pl.ds(t, S, stride=16), :]
        drift_row = jnp.where(sub8 == 0, jnp.broadcast_to(mean[t : t + 1, :], (8, 128)), 0.0)
        block = jnp.concatenate([field, drift_row], axis=0)
        base[t] = block
        both[t, 0:S, :] = field
        both[t, S : S + 24, :] = field[0:24]
        weight = water[s : s + 1, :].astype(F32) * (-1.0 / CELLS)
        high, low = split(field * weight)
        weighted[0:S, lanes_of(c, s)] = high
        weighted[S : 2 * S, lanes_of(c, s)] = low
        high, low = split(field)
        side_high[64 : 64 + S, lanes_of(c, s)] = high
        side_low[64 : 64 + S, lanes_of(c, s)] = low
        columns = jnp.where(lane56 == 64 + t, pltpu.roll(block, 64 + t, 1), columns)
        columns = jnp.where(lane56 == t, pltpu.roll(block, t + 1, 1), columns)
        shore = jnp.where(lane1 == t, pltpu.roll(weight, t, 1) if t else weight, shore)
        shore = jnp.where(lane1 == 64 + t, pltpu.roll(weight, 65 + t, 1), shore)
        if s == 0:
            up_out[c] = block
        if s == 7:
            down_out[c] = block
        ahead = jnp.where(lane56 == 127, 0.0, pltpu.roll(block, 127, 1))
        behind = jnp.where(lane56 == 0, 0.0, pltpu.roll(block, 1, 1))
        across = 0.5 * (ahead - behind)
        grad_y[t, 0:S, :] = across[0:S]
        grad_y[t, S : S + 24, :] = across[0:24]
        grad_y[t, 72:80, :] = across[S:56]
    side_out[...] = columns

    def slope(t, before, after):
        along = 0.5 * (after - before)
        grad_x[t, 0:S, :] = along[0:S]
        grad_x[t, S : S + 24, :] = along[0:24]
        grad_x[t, 72:80, :] = along[S:56]

    for c, s in INNER:
        slope(c * 8 + s, base[c * 8 + s - 1], base[c * 8 + s + 1])

    own = pltpu.roll(columns, 64, 1)
    high, low = split(own[0:S] * shore)
    weighted[0:S, seam_lanes] = jnp.concatenate([high, jnp.zeros((S, 128), BF16)], axis=1)
    weighted[S : 2 * S, seam_lanes] = jnp.concatenate([low, jnp.zeros((S, 128), BF16)], axis=1)
    second_half = lax.rem(lax.div(lane56, 8), 2) == 1
    own = jnp.where(second_half, own, pltpu.roll(own, 120, 1))
    seam_field[0:S, :] = own[0:S]
    seam_field[S : S + 24, :] = own[0:24]
    seam_field[72:80, :] = own[S:56]

    gram = dot_nt(weighted[...], side_high[...])
    gram = gram[0:S] + gram[S : 2 * S] + dot_nt(weighted[0:S, :], side_low[...])
    moments[432:480, :] = moments[432:480, :] - pltpu.roll(gram, 8, 1)
    moments[480:REGION, :] = jnp.zeros((REGION - 480, 128), F32)
    pl.semaphore_wait(barrier, GROUP - 1 + DEEP - 1 + 2)
    halo = copies(
        (up_out, down_out, side_out, side_out), (up_in, down_in, left_in, right_in), 0
    )
    for copy in halo:
        copy.start()
    plane_start(moments, part_a, 0, CHUNK)

    def pair_value(d, t, u0, u1, v0, v1):
        ahead = pl.ds(d, S)
        return (
            u0 * grad_x[t, ahead, :] + u1 * grad_y[t, ahead, :]
            + v0 * grad_x[t, 0:S, :] + v1 * grad_y[t, 0:S, :]
        )

    def store(rows, lanes, value):
        high, low = split(value)
        pair_high[rows, lanes] = high
        pair_low[rows, lanes] = low

    def pairs_of(grid_rows, together):
        def pair_block(first, carry):
            for s in grid_rows:
                u0, u1 = both[s, 0:S, :], both[8 + s, 0:S, :]
                slopes = [(grad_x[c * 8 + s, 0:S, :], grad_y[c * 8 + s, 0:S, :]) for c in range(2)]
                for k in range(together):
                    d = first + k
                    rows = pl.ds(pl.multiple_of(d * S, S), S)
                    ahead = pl.ds(d, S)
                    v0, v1 = both[s, ahead, :], both[8 + s, ahead, :]
                    for c in range(2):
                        t = c * 8 + s
                        value = (
                            u0 * grad_x[t, ahead, :] + u1 * grad_y[t, ahead, :]
                            + v0 * slopes[c][0] + v1 * slopes[c][1]
                        )
                        store(rows, lanes_of(c, s), value)
            return carry

        return pair_block

    def last_rows(lanes, value, minus):
        store(slice(1152, 1200), lanes, jnp.concatenate([value[0:24], minus[0:24]], axis=0))
        store(slice(1200, WIDE), lanes, jnp.concatenate([minus[24:48], jnp.zeros((56, 128), F32)], axis=0))

    def other_pairs(grid_rows):
        for s in grid_rows:
            u0, u1 = both[s, 0:S, :], both[8 + s, 0:S, :]
            v0, v1 = both[s, 24:72, :], both[8 + s, 24:72, :]
            m0, m1 = base[s, S : S + 1, :], base[8 + s, S : S + 1, :]
            for c in range(2):
                t = c * 8 + s
                store(slice(0, S), lanes_of(c, s), u0 * grad_x[t, 0:S, :] + u1 * grad_y[t, 0:S, :])
                minus = (
                    m0 * grad_x[t, 0:S, :] + m1 * grad_y[t, 0:S, :]
                    + u0 * grad_x[t, 72:73, :] + u1 * grad_y[t, 72:73, :]
                )
                back[t] = minus
                last_rows(lanes_of(c, s), pair_value(24, t, u0, u1, v0, v1), minus)

    def project(first, count, target):
        rows = slice(first, first + count)
        out = dot_nt(weighted[...], pair_high[rows, :])
        out = out[0:S] + out[S : 2 * S] + dot_nt(weighted[0:S, :], pair_low[rows, :])
        for k in range(count // 128):
            to = (first // 128 + k) % 5 * S
            target[to : to + S, :] = out[:, k * 128 : (k + 1) * 128]

    other_pairs(range(1, 7))
    pairs_of(range(1, 7), 1)(1, 0)
    lax.fori_loop(1, 12, lambda i, carry: pairs_of(range(1, 7), 2)(2 * i, carry), 0)

    for copy in halo:
        copy.wait_recv()
    for c in range(2):
        slope(c * 8, jnp.where(row == 0, 0.0, up_in[c]), base[c * 8 + 1])
        slope(c * 8 + 7, base[c * 8 + 6], jnp.where(row == ROWS - 1, 0.0, down_in[c]))
    from_left = jnp.where(col == 0, 0.0, left_in[...])
    from_right = jnp.where(col == COLS - 1, 0.0, right_in[...])
    change = jnp.where(lane56 < 64, -0.5 * from_left, 0.5 * from_right)
    seam_slope[0:S, :] = change[0:S]
    seam_slope[S : S + 24, :] = change[0:24]
    seam_slope[72:80, :] = change[S:56]
    seam = slice(SEAM * 128, (SEAM + 1) * 128)

    def seam_value(d):
        ahead = pl.ds(d, S)
        return seam_field[0:S, :] * seam_slope[ahead, :] + seam_field[ahead, :] * seam_slope[0:S, :]

    def outer_pairs(i, carry):
        for k in range(2):
            store(pl.ds(pl.multiple_of((2 * i + k) * S, S), S), seam, seam_value(2 * i + k))
        return pairs_of((0, 7), 2)(2 * i, carry)

    other_pairs((0, 7))
    minus = seam_field[72:73, :] * seam_slope[0:S, :] + seam_field[0:S, :] * seam_slope[72:73, :]
    seam_back[...] = minus
    store(slice(0, S), seam, seam_field[0:S, :] * seam_slope[0:S, :])
    last_rows(seam, seam_value(24), minus)
    pair_high[:, 17 * 128 : LANES] = jnp.zeros((WIDE, 128), BF16)
    pair_low[:, 17 * 128 : LANES] = jnp.zeros((WIDE, 128), BF16)
    store(slice(S, 2 * S), seam, seam_value(1))
    pairs_of((0, 7), 1)(1, 0)
    lax.fori_loop(1, 7, outer_pairs, 0)
    project(0, 256, tensor_b)
    project(256, 256, tensor_b)
    project(512, 128, tensor_b)
    tensor_b[240:HALF_REGION, :] = jnp.zeros((HALF_REGION - 240, 128), F32)
    plane_start(tensor_b, part_b, 3, HALF_CHUNK)
    deep_start(moments, part_a, mine_a, deep_a, 0, CHUNK)

    lax.fori_loop(7, 12, outer_pairs, 0)
    project(640, 128, tensor_c)
    project(768, 256, tensor_c)
    project(1024, 256, tensor_c)
    tensor_c[240:HALF_REGION, :] = jnp.zeros((HALF_REGION - 240, 128), F32)
    plane_start(tensor_c, part_c, 6, HALF_CHUNK)
    deep_start(tensor_b, part_b, mine_b, deep_b, 3, HALF_CHUNK)
    gather_start(mine_a, deep_a, total_a, 0, CHUNK)
    deep_start(tensor_c, part_c, mine_c, deep_c, 6, HALF_CHUNK)

    gather_start(mine_b, deep_b, total_b, 3, HALF_CHUNK)
    gather_start(mine_c, deep_c, total_c, 6, HALF_CHUNK)
    gather_wait(part_a, 0)
    tail = total_a[432:480, :]
    second = jnp.where(lane < S, pltpu.roll(tail, 128 - 24, 1), 0.0) * (1.0 / R)
    gram_inv[...] = jnp.where(lane < S, pltpu.roll(tail, 128 - 72, 1), 0.0)
    mean_col = jnp.sum(jnp.where(lane == 120, tail, 0.0), axis=1, keepdims=True) * (1.0 / R)
    mean_row = jnp.sum(jnp.where(lane == sub, mean_col, 0.0), axis=0, keepdims=True)
    cov_inv[...] = second - mean_col * mean_row
    for lb in range(10):
        number = lb * 128 + lane
        first_d = lb * 128 // S
        d = jnp.full((S, 128), first_d, jnp.int32)
        for step in range(first_d + 1, first_d + 4):
            d = d + jnp.where(number >= step * S, 1, 0)
        k = number - d * S
        l = k + d
        l = jnp.where(l >= S, l - S, l)
        hot_k = jnp.where(sub == k, 1.0, 0.0)
        hot_l = jnp.where(sub == l, 1.0, 0.0)
        at_k = exact(second, tall(hot_k))
        at_l = exact(second, tall(hot_l))
        mean_k = jnp.sum(mean_col * hot_k, axis=0, keepdims=True)
        mean_l = jnp.sum(mean_col * hot_l, axis=0, keepdims=True)
        second_kl = jnp.sum(hot_k * at_l, axis=0, keepdims=True)
        third = total_a[lb * S : (lb + 1) * S, :] * (1.0 / R)
        third = third - mean_col * (second_kl - 2.0 * (mean_k * mean_l)) - mean_k * at_l - mean_l * at_k
        cov = second_kl - mean_k * mean_l
        if lb == 9:
            third = jnp.where(lane < 24, third, 0.0)
            cov = jnp.where(lane1 < 24, cov, 0.0)
        cube[lb * S : (lb + 1) * S, :] = third
        high, low = split(third)
        cube_split[0:S, lb * 128 : (lb + 1) * 128] = high
        cube_split[S : 2 * S, lb * 128 : (lb + 1) * 128] = low
        pair_cov[lb : lb + 1, :] = cov

    def contract(n, carry):
        cells = pl.ds(pl.multiple_of(n * 256, 256), 256)
        out = dot(cube_split[...], pair_high[:, cells])
        out = out[0:S] + out[S : 2 * S] + dot(cube_split[0:S, :], pair_low[:, cells])
        high, low = split(out)
        side_high[0:S, cells] = high
        side_low[0:S, cells] = low
        return carry

    def picked(at, values, axis):
        return jnp.sum(jnp.where(at, values, 0.0), axis=axis, keepdims=True)

    def eliminate(i, carry):
        p = 2 * i
        for matrix in (cov_inv, gram_inv):
            value = matrix[...]
            line_p, line_q = matrix[pl.ds(p, 1), :], matrix[pl.ds(p + 1, 1), :]
            at_p, at_q = lane1 == p, lane1 == p + 1
            a, b, d = picked(at_p, line_p, 1), picked(at_q, line_p, 1), picked(at_q, line_q, 1)
            column_p, column_q = picked(lane == p, value, 1), picked(lane == p + 1, value, 1)
            inverse = 1.0 / a
            ratio = b * inverse
            g = 1.0 / (d - b * ratio)
            f = -ratio * g
            e = inverse - ratio * f
            new_p = jnp.where(at_p, e, jnp.where(at_q, f, e * line_p + f * line_q))
            new_q = jnp.where(at_p, f, jnp.where(at_q, g, f * line_p + g * line_q))
            value = jnp.where((lane == p) | (lane == p + 1), 0.0, value)
            value = value - column_p * new_p - column_q * new_q
            matrix[...] = jnp.where(sub == p, new_p, jnp.where(sub == p + 1, new_q, value))
        return carry

    def contract_and_eliminate(n, carry):
        contract(n, carry)
        for k in range(3):
            eliminate(n * 3 + k, carry)
        return carry

    lax.fori_loop(0, 8, contract_and_eliminate, 0)
    contract(8, 0)

    def split3(value):
        high, low = split(value)
        lowest = (value - high.astype(F32) - low.astype(F32)).astype(BF16)
        return jnp.concatenate([high, low, lowest], axis=0)

    from_cov = split3(cov_inv[...])
    from_gram = split3(pltpu.roll(gram_inv[...], 64, 1))
    out = dot(from_cov[:, 0:S], cube_split[0:S, :])
    rest = dot(from_cov[0 : 2 * S, 0:S], cube_split[S : 2 * S, :])
    keys = out[0:S] + out[S : 2 * S] + out[2 * S : 3 * S] + rest[0:S] + rest[S : 2 * S]
    for lb in range(10):
        value = keys[:, lb * 128 : (lb + 1) * 128]
        if lb == 9:
            value = jnp.where(lane == sub + 24, 1.0, value)
        high, low = split(value)
        key_high[0:S, lb * 128 : (lb + 1) * 128] = high
        key_low[0:S, lb * 128 : (lb + 1) * 128] = low
    key_high[S:128, :] = jnp.zeros((128 - S, WIDE), BF16)
    key_low[S:128, :] = jnp.zeros((128 - S, WIDE), BF16)

    def product(factors, cells):
        out = dot(factors, side_high[:, cells])
        rest = dot(factors[0 : 2 * S], side_low[:, cells])
        return out[0:S] + out[S : 2 * S] + out[2 * S : 3 * S] + rest[0:S] + rest[S : 2 * S]

    seam_part = product(from_cov, slice(2048, LANES))[:, 0:128] + seam_back[...]
    for n in range(8):
        cells = slice(n * 256, (n + 1) * 256)
        out = product(from_cov, cells)
        high, low = split(product(from_gram, cells))
        side_high[64 : 64 + S, cells] = high
        side_low[64 : 64 + S, cells] = low
        for k in range(2):
            c, s = (INNER + OUTER)[2 * n + k]
            t = c * 8 + s
            part = back[t] + out[:, k * 128 : (k + 1) * 128]
            at_left = pltpu.roll(seam_part, 128 - t, 1) if t else seam_part
            part = part + jnp.where(lane == 0, at_left, 0.0)
            part = part + jnp.where(lane == 127, pltpu.roll(seam_part, 63 - t, 1), 0.0)
            half[t] = both[t, 0:S, :] - STEP * part
    gather_wait(part_b, 3)
    gather_wait(part_c, 6)

    def summed(lb):
        return (total_b if lb < 5 else total_c)[lb % 5 * S : (lb % 5 + 1) * S, :]

    totals = split3(jnp.concatenate([summed(lb) for lb in range(10)], axis=1))
    out = dot_nt(totals, key_high[...])
    rest = dot_nt(totals[0 : 2 * S], key_low[...])
    out = out[0:S] + out[S : 2 * S] + out[2 * S : 3 * S] + rest[0:S] + rest[S : 2 * S]
    from_sums = split3(pltpu.roll(tall(out).T[0:S], 64, 1))
    halo2 = copies(
        (up_out2, down_out2, side_out2, side_out2), (up_in2, down_in2, left_in2, right_in2), 4
    )
    columns = jnp.zeros((S, 128), F32)
    for n in (6, 7, 0, 1, 2, 3, 4, 5):
        out = product(from_sums, slice(n * 256, (n + 1) * 256))
        for k in range(2):
            c, s = (INNER + OUTER)[2 * n + k]
            t = c * 8 + s
            value = half[t] - STEP * out[:, k * 128 : (k + 1) * 128]
            value = water[s : s + 1, :].astype(F32) * value
            half[t] = value
            columns = jnp.where(lane == 64 + t, pltpu.roll(value, 64 + t, 1), columns)
            columns = jnp.where(lane == t, pltpu.roll(value, t + 1, 1), columns)
            if s == 0:
                up_out2[c] = value
            if s == 7:
                down_out2[c] = value
        if n == 7:
            for copy in halo2[0:2]:
                copy.start()
    side_out2[...] = columns
    for copy in halo2[2:4]:
        copy.start()

    centred = raw - mean_col
    pair_up(centred, False)
    change = jnp.zeros((S, 128), F32)
    excess = jnp.zeros((S, 128), F32)
    for lb in range(10):
        here = summed(lb)
        change = change + exact(here, pair_coeffs[lb * 128 : (lb + 1) * 128, :])
        excess = excess + here * pair_cov[lb : lb + 1, :]
    change = change - jnp.sum(excess, axis=1, keepdims=True)
    new_coeffs[...] = centred + STEP * exact(gram_inv[...], tall(change))

    for copy in halo2:
        copy.wait_recv()
    from_left = jnp.where(col == 0, 0.0, left_in2[...])
    from_right = jnp.where(col == COLS - 1, 0.0, right_in2[...])
    for t in range(16):
        c, s = divmod(t, 8)
        value = half[t]
        before = jnp.where(row == 0, 0.0, up_in2[c]) if s == 0 else half[t - 1]
        after = jnp.where(row == ROWS - 1, 0.0, down_in2[c]) if s == 7 else half[t + 1]
        ahead = jnp.where(lane == 127, pltpu.roll(from_right, 63 - t, 1), pltpu.roll(value, 127, 1))
        shifted = pltpu.roll(from_left, 128 - t, 1) if t else from_left
        behind = jnp.where(lane == 0, shifted, pltpu.roll(value, 1, 1))
        laplace = after + before + ahead + behind - 4.0 * value
        mask = water[s : s + 1, :].astype(F32)
        new_modes[pl.ds(t, S, stride=16), :] = mask * (value + VISCOUS * laplace)

    for copy in halo + halo2:
        copy.wait_send()
    sums_sent(part_a, deep_a, 0)
    sums_sent(part_b, deep_b, 3)
    sums_sent(part_c, deep_c, 6)


def on_device(modes, mean_flow, seeds, amplitudes, water_mask):
    vmem = pl.BlockSpec(memory_space=pltpu.VMEM)

    def f32(*shape):
        return pltpu.VMEM(shape, F32)

    def bf16(*shape):
        return pltpu.VMEM(shape, BF16)

    def sums(chunk):
        return [
            f32((GROUP - 1) * chunk, 128), f32((DEEP - 1) * chunk, 128), f32(2 * chunk, 128), f32(GROUP * chunk, 128)
        ]

    new_modes, new_coeffs = pl.pallas_call(
        kernel,
        out_shape=(
            jax.ShapeDtypeStruct((S * 16, 128), F32),
            jax.ShapeDtypeStruct((S, 128), F32),
        ),
        in_specs=[pl.BlockSpec(memory_space=pltpu.MemorySpace.HBM)] * 5,
        out_specs=(vmem, vmem),
        scratch_shapes=[
            f32(S * 16, 128), f32(16, 128), pltpu.VMEM((S, 128), jnp.int32), f32(1, S), pltpu.VMEM((8, 128), jnp.int32),
            f32(16, 56, 128), f32(16, 72, 128), f32(16, 80, 128), f32(16, 80, 128), f32(16, S, 128),
            bf16(2 * S, LANES), bf16(WIDE, LANES), bf16(WIDE, LANES), bf16(128, LANES), bf16(128, LANES),
            f32(80, 128), f32(80, 128), f32(S, 128), f32(8, 128), f32(72, 128), f32(WIDE, 128),
            f32(REGION, 128), f32(HALF_REGION, 128), f32(HALF_REGION, 128), f32(480, 128), bf16(2 * S, WIDE),
            f32(16, 128), f32(S, 128), f32(S, 128), f32(16, S, 128), bf16(128, WIDE), bf16(128, WIDE),
            *sums(CHUNK), *sums(HALF_CHUNK), *sums(HALF_CHUNK),
            f32(2, 56, 128), f32(2, 56, 128), f32(56, 128), f32(2, 56, 128), f32(2, 56, 128), f32(56, 128), f32(56, 128),
            f32(2, S, 128), f32(2, S, 128), f32(S, 128), f32(2, S, 128), f32(2, S, 128), f32(S, 128), f32(S, 128),
            pltpu.SemaphoreType.DMA((8,)), pltpu.SemaphoreType.DMA((8,)),
            pltpu.SemaphoreType.DMA((9,)), pltpu.SemaphoreType.DMA((9,)), pltpu.SemaphoreType.DMA((5,)),
        ],
        compiler_params=pltpu.CompilerParams(
            collective_id=0, has_side_effects=True, vmem_limit_bytes=32 * 1024 * 1024
        ),
    )(
        *(
            pltpu.with_memory_space_constraint(value, pltpu.MemorySpace.HBM)
            for value in (
                modes.reshape(S * 16, 128),
                mean_flow.reshape(16, 128),
                seeds.T,
                amplitudes.reshape(1, S),
                water_mask,
            )
        )
    )
    return new_modes.reshape(S, 2, 8, 128), new_coeffs.T


def solution(mesh):
    return jax.shard_map(
        on_device,
        mesh=mesh,
        in_specs=(
            P(None, None, "row", "col"),
            P(None, "row", "col"),
            P(("row", "col"), None),
            P(),
            P("row", "col"),
        ),
        out_specs=(P(None, None, "row", "col"), P(("row", "col"), None)),
        check_vma=False,
    )
```

```python
import math

import jax
import jax.numpy as jnp
from jax import lax
from jax.experimental import pallas as pl
from jax.experimental.pallas import tpu as pltpu
from jax.sharding import PartitionSpec as P

F32 = jnp.float32
BF16 = jnp.bfloat16
MESH = pl.DeviceIdType.MESH
HIGHEST = lax.Precision.HIGHEST

S = 48
R = 32768
CELLS = 2.0 * 64 * 4096
STEP = 0.25
VISCOUS = 0.2
ROWS, COLS, ALONG_X = 8, 32, 4
GROUP = ROWS * ALONG_X
DEEP = COLS // ALONG_X
CHUNK = 16
REGION = GROUP * CHUNK
HALF_CHUNK = CHUNK // 2
HALF_REGION = GROUP * HALF_CHUNK
PAIRS = 1176
WIDE = 1280
INNER = [(c, s) for s in range(1, 7) for c in range(2)]
OUTER = [(c, s) for s in (0, 7) for c in range(2)]
SLOT = {place: number for number, place in enumerate(INNER + OUTER)}
SEAM = 16
LANES = 18 * 128
NT = (((1,), (1,)), ((), ()))


def split(value):
    high = value.astype(BF16)
    return high, (value - high.astype(F32)).astype(BF16)


def dot(a, b):
    return jnp.dot(a, b, preferred_element_type=F32)


def dot_nt(a, b):
    return lax.dot_general(a, b, NT, preferred_element_type=F32)


def exact(a, b):
    return jnp.dot(a, b, precision=HIGHEST, preferred_element_type=F32)


def exact_nt(a, b):
    return lax.dot_general(a, b, NT, precision=HIGHEST, preferred_element_type=F32)


def tall(value):
    return jnp.concatenate([value, jnp.zeros((128 - S, 128), F32)], axis=0)


def kernel(
    modes_hbm, mean_hbm, seeds_hbm, amps_hbm, water_hbm, new_modes, new_coeffs,
    modes, mean, seeds, amps, water,
    base, both, grad_x, grad_y, back, weighted, pair_high, pair_low, side_high, side_low,
    seam_field, seam_slope, seam_back, amp_row, coeffs, pair_coeffs, moments, tensor_b, tensor_c, cube, cube_split, pair_cov,
    cov_inv, gram_inv, half, key_high, key_low,
    part_a, deep_a, mine_a, total_a, part_b, deep_b, mine_b, total_b, part_c, deep_c, mine_c, total_c,
    up_out, down_out, side_out, up_in, down_in, left_in, right_in,
    up_out2, down_out2, side_out2, up_in2, down_in2, left_in2, right_in2,
    halo_send, halo_recv, sum_send, sum_recv, fetch_sem,
):
    row = lax.axis_index("row")
    col = lax.axis_index("col")
    along_x = lax.rem(col, ALONG_X)
    plane = lax.div(col, ALONG_X)
    place = row * ALONG_X + along_x
    above = lax.rem(row + ROWS - 1, ROWS)
    below = lax.rem(row + 1, ROWS)
    left = lax.rem(col + COLS - 1, COLS)
    right = lax.rem(col + 1, COLS)

    def member(offset):
        other = lax.rem(place + offset, GROUP)
        return other, (lax.div(other, ALONG_X), plane * ALONG_X + lax.rem(other, ALONG_X))

    def deep(offset):
        return (row, lax.rem(plane + offset, DEEP) * ALONG_X + along_x)

    barrier = pltpu.get_barrier_semaphore()

    def greet_plane(offset, carry):
        pl.semaphore_signal(barrier, inc=1, device_id=member(offset)[1], device_id_type=MESH)
        return carry

    def greet_deep(offset, carry):
        pl.semaphore_signal(barrier, inc=1, device_id=deep(offset), device_id_type=MESH)
        return carry

    for offset in range(1, GROUP):
        greet_plane(offset, 0)
    for offset in range(1, DEEP):
        greet_deep(offset, 0)
    pl.semaphore_signal(barrier, inc=1, device_id=(row, left), device_id_type=MESH)
    pl.semaphore_signal(barrier, inc=1, device_id=(row, right), device_id_type=MESH)

    fetches = [
        pltpu.make_async_copy(source, target, fetch_sem.at[k])
        for k, (source, target) in enumerate(
            ((seeds_hbm, seeds), (amps_hbm, amps), (modes_hbm, modes), (mean_hbm, mean), (water_hbm, water))
        )
    ]
    for fetch in fetches:
        fetch.start()

    lane = lax.broadcasted_iota(jnp.int32, (S, 128), 1)
    lane1 = lax.broadcasted_iota(jnp.int32, (1, 128), 1)
    sub = lax.broadcasted_iota(jnp.int32, (S, 128), 0)
    sub8 = lax.broadcasted_iota(jnp.int32, (8, 128), 0)

    def copies(outs, ins, first):
        targets = ((above, col), (below, col), (row, left), (row, right))
        arrivals = (ins[1], ins[0], ins[3], ins[2])
        return [
            pltpu.make_async_remote_copy(
                src_ref=outs[k],
                dst_ref=arrivals[k],
                send_sem=halo_send.at[first + k],
                recv_sem=halo_recv.at[first + k],
                device_id=targets[k],
                device_id_type=MESH,
            )
            for k in range(4)
        ]

    def plane_start(source, parts, sems, chunk):
        def send(offset, carry):
            other, device = member(offset)
            pltpu.make_async_remote_copy(
                src_ref=source.at[pl.ds(pl.multiple_of(other * chunk, chunk), chunk)],
                dst_ref=parts.at[pl.ds(pl.multiple_of((offset - 1) * chunk, chunk), chunk)],
                send_sem=sum_send.at[sems],
                recv_sem=sum_recv.at[sems],
                device_id=device,
                device_id_type=MESH,
            ).start()
            return carry

        for offset in range(1, GROUP):
            send(offset, 0)

    def deep_start(source, parts, mine, deeper, sems, chunk):
        pltpu.make_async_copy(parts, parts, sum_recv.at[sems]).wait()
        value = source[pl.ds(pl.multiple_of(place * chunk, chunk), chunk), :]
        for k in range(GROUP - 1):
            value = value + parts[k * chunk : (k + 1) * chunk, :]
        mine[0:chunk, :] = value

        def send(offset, carry):
            pltpu.make_async_remote_copy(
                src_ref=mine.at[pl.ds(0, chunk)],
                dst_ref=deeper.at[pl.ds(pl.multiple_of((offset - 1) * chunk, chunk), chunk)],
                send_sem=sum_send.at[sems + 1],
                recv_sem=sum_recv.at[sems + 1],
                device_id=deep(offset),
                device_id_type=MESH,
            ).start()
            return carry

        for offset in range(1, DEEP):
            send(offset, 0)

    def gather_start(mine, deeper, total, sems, chunk):
        pltpu.make_async_copy(deeper, deeper, sum_recv.at[sems + 1]).wait()
        value = mine[0:chunk, :]
        for k in range(DEEP - 1):
            value = value + deeper[k * chunk : (k + 1) * chunk, :]
        mine[chunk : 2 * chunk, :] = value
        own = pl.ds(pl.multiple_of(place * chunk, chunk), chunk)
        total[own, :] = value

        def send(offset, carry):
            pltpu.make_async_remote_copy(
                src_ref=mine.at[pl.ds(chunk, chunk)],
                dst_ref=total.at[own],
                send_sem=sum_send.at[sems + 2],
                recv_sem=sum_recv.at[sems + 2],
                device_id=member(offset)[1],
                device_id_type=MESH,
            ).start()
            return carry

        for offset in range(1, GROUP):
            send(offset, 0)

    def gather_wait(parts, sems):
        pltpu.make_async_copy(parts, parts, sum_recv.at[sems + 2]).wait()

    def sums_sent(parts, deeper, sems):
        pltpu.make_async_copy(parts, parts, sum_send.at[sems]).wait()
        pltpu.make_async_copy(deeper, deeper, sum_send.at[sems + 1]).wait()
        pltpu.make_async_copy(parts, parts, sum_send.at[sems + 2]).wait()

    for fetch in fetches[:2]:
        fetch.wait()
    phase = seeds[...].astype(F32) * (3.0 * math.pi / 8192.0)
    wave = jnp.cos(phase)
    strength = 0.5 + ((row * COLS + col) * 128 + lane).astype(F32) * (1.0 / R)
    amp_row[...] = jnp.zeros((8, 128), F32)
    amp_row[0:1, 0:S] = amps[...]
    amp_col = jnp.sum(jnp.where(lane == sub, amp_row[0:1, :], 0.0), axis=1, keepdims=True)
    raw = strength * amp_col * (wave + (wave * wave - 0.5))

    def pair_up(values, ones):
        coeffs[0:S, :] = values
        coeffs[S : S + 24, :] = values[0:24]
        for d in range(24):
            pair_coeffs[d * S : (d + 1) * S, :] = values * coeffs[d : d + S, :]
        pair_coeffs[1152:PAIRS, :] = values[0:24] * coeffs[24:48, :]
        pair_coeffs[PAIRS : PAIRS + S, :] = values
        pair_coeffs[PAIRS + S : WIDE, :] = jnp.zeros((WIDE - PAIRS - S, 128), F32)
        if ones:
            pair_coeffs[1272:1280, :] = jnp.where(sub8 == 0, 1.0, 0.0)

    pair_up(raw, True)
    for lb in range(5):
        out = exact_nt(raw, pair_coeffs[lb * 256 : (lb + 1) * 256, :])
        moments[lb * 96 : lb * 96 + S, :] = out[:, 0:128]
        moments[lb * 96 + S : lb * 96 + 96, :] = out[:, 128:256]
    for fetch in fetches[2:]:
        fetch.wait()

    def lanes_of(c, s):
        return slice(SLOT[c, s] * 128, (SLOT[c, s] + 1) * 128)

    seam_lanes = slice(SEAM * 128, LANES)
    side_high[...] = jnp.zeros((128, LANES), BF16)
    side_low[...] = jnp.zeros((128, LANES), BF16)
    lane56 = lax.broadcasted_iota(jnp.int32, (56, 128), 1)
    columns = jnp.zeros((56, 128), F32)
    shore = jnp.zeros((1, 128), F32)
    for t in range(16):
        c, s = divmod(t, 8)
        field = modes[pl.ds(t, S, stride=16), :]
        drift_row = jnp.where(sub8 == 0, jnp.broadcast_to(mean[t : t + 1, :], (8, 128)), 0.0)
        block = jnp.concatenate([field, drift_row], axis=0)
        base[t] = block
        both[t, 0:S, :] = field
        both[t, S : S + 24, :] = field[0:24]
        weight = water[s : s + 1, :].astype(F32) * (-1.0 / CELLS)
        high, low = split(field * weight)
        weighted[0:S, lanes_of(c, s)] = high
        weighted[S : 2 * S, lanes_of(c, s)] = low
        high, low = split(field)
        side_high[64 : 64 + S, lanes_of(c, s)] = high
        side_low[64 : 64 + S, lanes_of(c, s)] = low
        columns = jnp.where(lane56 == 64 + t, pltpu.roll(block, 64 + t, 1), columns)
        columns = jnp.where(lane56 == t, pltpu.roll(block, t + 1, 1), columns)
        shore = jnp.where(lane1 == t, pltpu.roll(weight, t, 1) if t else weight, shore)
        shore = jnp.where(lane1 == 64 + t, pltpu.roll(weight, 65 + t, 1), shore)
        if s == 0:
            up_out[c] = block
        if s == 7:
            down_out[c] = block
        ahead = jnp.where(lane56 == 127, 0.0, pltpu.roll(block, 127, 1))
        behind = jnp.where(lane56 == 0, 0.0, pltpu.roll(block, 1, 1))
        across = 0.5 * (ahead - behind)
        grad_y[t, 0:S, :] = across[0:S]
        grad_y[t, S : S + 24, :] = across[0:24]
        grad_y[t, 72:80, :] = across[S:56]
    side_out[...] = columns

    def slope(t, before, after):
        along = 0.5 * (after - before)
        grad_x[t, 0:S, :] = along[0:S]
        grad_x[t, S : S + 24, :] = along[0:24]
        grad_x[t, 72:80, :] = along[S:56]

    for c, s in INNER:
        slope(c * 8 + s, base[c * 8 + s - 1], base[c * 8 + s + 1])

    own = pltpu.roll(columns, 64, 1)
    high, low = split(own[0:S] * shore)
    weighted[0:S, seam_lanes] = jnp.concatenate([high, jnp.zeros((S, 128), BF16)], axis=1)
    weighted[S : 2 * S, seam_lanes] = jnp.concatenate([low, jnp.zeros((S, 128), BF16)], axis=1)
    second_half = lax.rem(lax.div(lane56, 8), 2) == 1
    own = jnp.where(second_half, own, pltpu.roll(own, 120, 1))
    seam_field[0:S, :] = own[0:S]
    seam_field[S : S + 24, :] = own[0:24]
    seam_field[72:80, :] = own[S:56]

    gram = dot_nt(weighted[...], side_high[...])
    gram = gram[0:S] + gram[S : 2 * S] + dot_nt(weighted[0:S, :], side_low[...])
    moments[432:480, :] = moments[432:480, :] - pltpu.roll(gram, 8, 1)
    moments[480:REGION, :] = jnp.zeros((REGION - 480, 128), F32)
    pl.semaphore_wait(barrier, GROUP - 1 + DEEP - 1 + 2)
    halo = copies(
        (up_out, down_out, side_out, side_out), (up_in, down_in, left_in, right_in), 0
    )
    for copy in halo:
        copy.start()
    plane_start(moments, part_a, 0, CHUNK)

    def pair_value(d, t, u0, u1, v0, v1):
        ahead = pl.ds(d, S)
        return (
            u0 * grad_x[t, ahead, :] + u1 * grad_y[t, ahead, :]
            + v0 * grad_x[t, 0:S, :] + v1 * grad_y[t, 0:S, :]
        )

    def store(rows, lanes, value):
        high, low = split(value)
        pair_high[rows, lanes] = high
        pair_low[rows, lanes] = low

    def block_rows(d):
        return slice(d * S, (d + 1) * S) if isinstance(d, int) else pl.ds(pl.multiple_of(d * S, S), S)

    def pairs_of(grid_rows, together):
        def pair_block(first, carry):
            for s in grid_rows:
                u0, u1 = both[s, 0:S, :], both[8 + s, 0:S, :]
                slopes = [(grad_x[c * 8 + s, 0:S, :], grad_y[c * 8 + s, 0:S, :]) for c in range(2)]
                for k in range(together):
                    d = first + k
                    rows = block_rows(d)
                    ahead = pl.ds(d, S)
                    v0, v1 = both[s, ahead, :], both[8 + s, ahead, :]
                    for c in range(2):
                        t = c * 8 + s
                        value = (
                            u0 * grad_x[t, ahead, :] + u1 * grad_y[t, ahead, :]
                            + v0 * slopes[c][0] + v1 * slopes[c][1]
                        )
                        store(rows, lanes_of(c, s), value)
            return carry

        return pair_block

    def last_rows(lanes, value, minus):
        store(slice(1152, 1200), lanes, jnp.concatenate([value[0:24], minus[0:24]], axis=0))
        store(slice(1200, WIDE), lanes, jnp.concatenate([minus[24:48], jnp.zeros((56, 128), F32)], axis=0))

    def other_pairs(grid_rows):
        for s in grid_rows:
            u0, u1 = both[s, 0:S, :], both[8 + s, 0:S, :]
            v0, v1 = both[s, 24:72, :], both[8 + s, 24:72, :]
            m0, m1 = base[s, S : S + 1, :], base[8 + s, S : S + 1, :]
            for c in range(2):
                t = c * 8 + s
                store(slice(0, S), lanes_of(c, s), u0 * grad_x[t, 0:S, :] + u1 * grad_y[t, 0:S, :])
                minus = (
                    m0 * grad_x[t, 0:S, :] + m1 * grad_y[t, 0:S, :]
                    + u0 * grad_x[t, 72:73, :] + u1 * grad_y[t, 72:73, :]
                )
                back[t] = minus
                last_rows(lanes_of(c, s), pair_value(24, t, u0, u1, v0, v1), minus)

    def project(first, count, target):
        rows = slice(first, first + count)
        out = dot_nt(weighted[...], pair_high[rows, :])
        out = out[0:S] + out[S : 2 * S] + dot_nt(weighted[0:S, :], pair_low[rows, :])
        for k in range(count // 128):
            to = (first // 128 + k) % 5 * S
            target[to : to + S, :] = out[:, k * 128 : (k + 1) * 128]

    other_pairs(range(1, 7))
    pairs_of(range(1, 7), 1)(1, 0)
    lax.fori_loop(1, 12, lambda i, carry: pairs_of(range(1, 7), 2)(2 * i, carry), 0)

    for copy in halo:
        copy.wait_recv()
    for c in range(2):
        slope(c * 8, jnp.where(row == 0, 0.0, up_in[c]), base[c * 8 + 1])
        slope(c * 8 + 7, base[c * 8 + 6], jnp.where(row == ROWS - 1, 0.0, down_in[c]))
    from_left = jnp.where(col == 0, 0.0, left_in[...])
    from_right = jnp.where(col == COLS - 1, 0.0, right_in[...])
    change = jnp.where(lane56 < 64, -0.5 * from_left, 0.5 * from_right)
    seam_slope[0:S, :] = change[0:S]
    seam_slope[S : S + 24, :] = change[0:24]
    seam_slope[72:80, :] = change[S:56]
    seam = slice(SEAM * 128, (SEAM + 1) * 128)

    def seam_value(d):
        ahead = pl.ds(d, S)
        return seam_field[0:S, :] * seam_slope[ahead, :] + seam_field[ahead, :] * seam_slope[0:S, :]

    def outer_pairs(i, carry):
        for k in range(2):
            store(block_rows(2 * i + k), seam, seam_value(2 * i + k))
        return pairs_of((0, 7), 2)(2 * i, carry)

    other_pairs((0, 7))
    minus = seam_field[72:73, :] * seam_slope[0:S, :] + seam_field[0:S, :] * seam_slope[72:73, :]
    seam_back[...] = minus
    store(slice(0, S), seam, seam_field[0:S, :] * seam_slope[0:S, :])
    last_rows(seam, seam_value(24), minus)
    pair_high[:, 17 * 128 : LANES] = jnp.zeros((WIDE, 128), BF16)
    pair_low[:, 17 * 128 : LANES] = jnp.zeros((WIDE, 128), BF16)
    store(slice(S, 2 * S), seam, seam_value(1))
    pairs_of((0, 7), 1)(1, 0)
    lax.fori_loop(1, 7, outer_pairs, 0)
    project(0, 256, tensor_b)
    project(256, 256, tensor_b)
    project(512, 128, tensor_b)
    for i in range(7, 12):
        outer_pairs(i, 0)
    tensor_b[240:HALF_REGION, :] = jnp.zeros((HALF_REGION - 240, 128), F32)
    plane_start(tensor_b, part_b, 3, HALF_CHUNK)
    deep_start(moments, part_a, mine_a, deep_a, 0, CHUNK)

    project(640, 128, tensor_c)
    project(768, 256, tensor_c)
    project(1024, 256, tensor_c)
    tensor_c[240:HALF_REGION, :] = jnp.zeros((HALF_REGION - 240, 128), F32)
    plane_start(tensor_c, part_c, 6, HALF_CHUNK)
    deep_start(tensor_b, part_b, mine_b, deep_b, 3, HALF_CHUNK)
    gather_start(mine_a, deep_a, total_a, 0, CHUNK)
    deep_start(tensor_c, part_c, mine_c, deep_c, 6, HALF_CHUNK)

    gather_start(mine_b, deep_b, total_b, 3, HALF_CHUNK)
    gather_start(mine_c, deep_c, total_c, 6, HALF_CHUNK)
    gather_wait(part_a, 0)
    tail = total_a[432:480, :]
    second = jnp.where(lane < S, pltpu.roll(tail, 128 - 24, 1), 0.0) * (1.0 / R)
    gram_inv[...] = jnp.where(lane < S, pltpu.roll(tail, 128 - 72, 1), 0.0)
    mean_col = jnp.sum(jnp.where(lane == 120, tail, 0.0), axis=1, keepdims=True) * (1.0 / R)
    mean_row = jnp.sum(jnp.where(lane == sub, mean_col, 0.0), axis=0, keepdims=True)
    cov_inv[...] = second - mean_col * mean_row
    def split3(value):
        high, low = split(value)
        lowest = (value - high.astype(F32) - low.astype(F32)).astype(BF16)
        return jnp.concatenate([high, low, lowest], axis=0)

    spread = split3(second)
    for lb in range(10):
        number = lb * 128 + lane
        first_d = lb * 128 // S
        d = jnp.full((S, 128), first_d, jnp.int32)
        for step in range(first_d + 1, first_d + 4):
            d = d + jnp.where(number >= step * S, 1, 0)
        k = number - d * S
        l = k + d
        l = jnp.where(l >= S, l - S, l)
        hot_k = jnp.where(sub == k, 1.0, 0.0)
        hot_l = jnp.where(sub == l, 1.0, 0.0)
        hot = jnp.concatenate([tall(hot_k), tall(hot_l)], axis=1).astype(BF16)
        out = dot(spread, hot)
        out = out[0:S] + out[S : 2 * S] + out[2 * S : 3 * S]
        at_k, at_l = out[:, 0:128], out[:, 128:256]
        mean_k = jnp.sum(mean_col * hot_k, axis=0, keepdims=True)
        mean_l = jnp.sum(mean_col * hot_l, axis=0, keepdims=True)
        second_kl = jnp.sum(hot_k * at_l, axis=0, keepdims=True)
        third = total_a[lb * S : (lb + 1) * S, :] * (1.0 / R)
        third = third - mean_col * (second_kl - 2.0 * (mean_k * mean_l)) - mean_k * at_l - mean_l * at_k
        cov = second_kl - mean_k * mean_l
        if lb == 9:
            third = jnp.where(lane < 24, third, 0.0)
            cov = jnp.where(lane1 < 24, cov, 0.0)
        cube[lb * S : (lb + 1) * S, :] = third
        high, low = split(third)
        cube_split[0:S, lb * 128 : (lb + 1) * 128] = high
        cube_split[S : 2 * S, lb * 128 : (lb + 1) * 128] = low
        pair_cov[lb : lb + 1, :] = cov

    def contract(n, carry):
        cells = pl.ds(pl.multiple_of(n * 256, 256), 256)
        out = dot(cube_split[...], pair_high[:, cells])
        out = out[0:S] + out[S : 2 * S] + dot(cube_split[0:S, :], pair_low[:, cells])
        high, low = split(out)
        side_high[0:S, cells] = high
        side_low[0:S, cells] = low
        return carry

    def picked(at, values, axis):
        return jnp.sum(jnp.where(at, values, 0.0), axis=axis, keepdims=True)

    def eliminate(i, carry):
        p = 2 * i
        for matrix in (cov_inv, gram_inv):
            value = matrix[...]
            line_p, line_q = matrix[pl.ds(p, 1), :], matrix[pl.ds(p + 1, 1), :]
            at_p, at_q = lane1 == p, lane1 == p + 1
            a, b, d = picked(at_p, line_p, 1), picked(at_q, line_p, 1), picked(at_q, line_q, 1)
            column_p, column_q = picked(lane == p, value, 1), picked(lane == p + 1, value, 1)
            inverse = 1.0 / a
            ratio = b * inverse
            g = 1.0 / (d - b * ratio)
            f = -ratio * g
            e = inverse - ratio * f
            new_p = jnp.where(at_p, e, jnp.where(at_q, f, e * line_p + f * line_q))
            new_q = jnp.where(at_p, f, jnp.where(at_q, g, f * line_p + g * line_q))
            value = jnp.where((lane == p) | (lane == p + 1), 0.0, value)
            value = value - column_p * new_p - column_q * new_q
            matrix[...] = jnp.where(sub == p, new_p, jnp.where(sub == p + 1, new_q, value))
        return carry

    def contract_and_eliminate(n, carry):
        contract(n, carry)
        for k in range(3):
            eliminate(n * 3 + k, carry)
        return carry

    lax.fori_loop(0, 8, contract_and_eliminate, 0)
    contract(8, 0)

    from_cov = split3(cov_inv[...])
    from_gram = split3(pltpu.roll(gram_inv[...], 64, 1))
    out = dot(from_cov[:, 0:S], cube_split[0:S, :])
    rest = dot(from_cov[0 : 2 * S, 0:S], cube_split[S : 2 * S, :])
    keys = out[0:S] + out[S : 2 * S] + out[2 * S : 3 * S] + rest[0:S] + rest[S : 2 * S]
    for lb in range(10):
        value = keys[:, lb * 128 : (lb + 1) * 128]
        if lb == 9:
            value = jnp.where(lane == sub + 24, 1.0, value)
        high, low = split(value)
        key_high[0:S, lb * 128 : (lb + 1) * 128] = high
        key_low[0:S, lb * 128 : (lb + 1) * 128] = low
    key_high[S:128, :] = jnp.zeros((128 - S, WIDE), BF16)
    key_low[S:128, :] = jnp.zeros((128 - S, WIDE), BF16)

    def product(factors, cells):
        out = dot(factors, side_high[:, cells])
        rest = dot(factors[0 : 2 * S], side_low[:, cells])
        return out[0:S] + out[S : 2 * S] + out[2 * S : 3 * S] + rest[0:S] + rest[S : 2 * S]

    seam_part = product(from_cov, slice(2048, LANES))[:, 0:128] + seam_back[...]
    for n in range(8):
        cells = slice(n * 256, (n + 1) * 256)
        out = product(from_cov, cells)
        high, low = split(product(from_gram, cells))
        side_high[64 : 64 + S, cells] = high
        side_low[64 : 64 + S, cells] = low
        for k in range(2):
            c, s = (INNER + OUTER)[2 * n + k]
            t = c * 8 + s
            part = back[t] + out[:, k * 128 : (k + 1) * 128]
            at_left = pltpu.roll(seam_part, 128 - t, 1) if t else seam_part
            part = part + jnp.where(lane == 0, at_left, 0.0)
            part = part + jnp.where(lane == 127, pltpu.roll(seam_part, 63 - t, 1), 0.0)
            half[t] = both[t, 0:S, :] - STEP * part
    gather_wait(part_b, 3)
    gather_wait(part_c, 6)

    def summed(lb):
        return (total_b if lb < 5 else total_c)[lb % 5 * S : (lb % 5 + 1) * S, :]

    totals = split3(jnp.concatenate([summed(lb) for lb in range(10)], axis=1))
    out = dot_nt(totals, key_high[...])
    rest = dot_nt(totals[0 : 2 * S], key_low[...])
    out = out[0:S] + out[S : 2 * S] + out[2 * S : 3 * S] + rest[0:S] + rest[S : 2 * S]
    from_sums = split3(pltpu.roll(tall(out).T[0:S], 64, 1))
    halo2 = copies(
        (up_out2, down_out2, side_out2, side_out2), (up_in2, down_in2, left_in2, right_in2), 4
    )
    columns = jnp.zeros((S, 128), F32)
    for n in (6, 7, 0, 1, 2, 3, 4, 5):
        out = product(from_sums, slice(n * 256, (n + 1) * 256))
        for k in range(2):
            c, s = (INNER + OUTER)[2 * n + k]
            t = c * 8 + s
            value = half[t] - STEP * out[:, k * 128 : (k + 1) * 128]
            value = water[s : s + 1, :].astype(F32) * value
            half[t] = value
            columns = jnp.where(lane == 64 + t, pltpu.roll(value, 64 + t, 1), columns)
            columns = jnp.where(lane == t, pltpu.roll(value, t + 1, 1), columns)
            if s == 0:
                up_out2[c] = value
            if s == 7:
                down_out2[c] = value
        if n == 7:
            for copy in halo2[0:2]:
                copy.start()
    side_out2[...] = columns
    for copy in halo2[2:4]:
        copy.start()

    centred = raw - mean_col
    pair_up(centred, False)
    change = jnp.zeros((S, 128), F32)
    excess = jnp.zeros((S, 128), F32)
    for lb in range(10):
        here = summed(lb)
        change = change + exact(here, pair_coeffs[lb * 128 : (lb + 1) * 128, :])
        excess = excess + here * pair_cov[lb : lb + 1, :]
    change = change - jnp.sum(excess, axis=1, keepdims=True)
    new_coeffs[...] = centred + STEP * exact(gram_inv[...], tall(change))

    for copy in halo2:
        copy.wait_recv()
    from_left = jnp.where(col == 0, 0.0, left_in2[...])
    from_right = jnp.where(col == COLS - 1, 0.0, right_in2[...])
    for t in range(16):
        c, s = divmod(t, 8)
        value = half[t]
        before = jnp.where(row == 0, 0.0, up_in2[c]) if s == 0 else half[t - 1]
        after = jnp.where(row == ROWS - 1, 0.0, down_in2[c]) if s == 7 else half[t + 1]
        ahead = jnp.where(lane == 127, pltpu.roll(from_right, 63 - t, 1), pltpu.roll(value, 127, 1))
        shifted = pltpu.roll(from_left, 128 - t, 1) if t else from_left
        behind = jnp.where(lane == 0, shifted, pltpu.roll(value, 1, 1))
        laplace = after + before + ahead + behind - 4.0 * value
        mask = water[s : s + 1, :].astype(F32)
        new_modes[pl.ds(t, S, stride=16), :] = mask * (value + VISCOUS * laplace)

    for copy in halo + halo2:
        copy.wait_send()
    sums_sent(part_a, deep_a, 0)
    sums_sent(part_b, deep_b, 3)
    sums_sent(part_c, deep_c, 6)


def on_device(modes, mean_flow, seeds, amplitudes, water_mask):
    vmem = pl.BlockSpec(memory_space=pltpu.VMEM)

    def f32(*shape):
        return pltpu.VMEM(shape, F32)

    def bf16(*shape):
        return pltpu.VMEM(shape, BF16)

    def sums(chunk):
        return [
            f32((GROUP - 1) * chunk, 128), f32((DEEP - 1) * chunk, 128), f32(2 * chunk, 128), f32(GROUP * chunk, 128)
        ]

    new_modes, new_coeffs = pl.pallas_call(
        kernel,
        out_shape=(
            jax.ShapeDtypeStruct((S * 16, 128), F32),
            jax.ShapeDtypeStruct((S, 128), F32),
        ),
        in_specs=[pl.BlockSpec(memory_space=pltpu.MemorySpace.HBM)] * 5,
        out_specs=(vmem, vmem),
        scratch_shapes=[
            f32(S * 16, 128), f32(16, 128), pltpu.VMEM((S, 128), jnp.int32), f32(1, S), pltpu.VMEM((8, 128), jnp.int32),
            f32(16, 56, 128), f32(16, 72, 128), f32(16, 80, 128), f32(16, 80, 128), f32(16, S, 128),
            bf16(2 * S, LANES), bf16(WIDE, LANES), bf16(WIDE, LANES), bf16(128, LANES), bf16(128, LANES),
            f32(80, 128), f32(80, 128), f32(S, 128), f32(8, 128), f32(72, 128), f32(WIDE, 128),
            f32(REGION, 128), f32(HALF_REGION, 128), f32(HALF_REGION, 128), f32(480, 128), bf16(2 * S, WIDE),
            f32(16, 128), f32(S, 128), f32(S, 128), f32(16, S, 128), bf16(128, WIDE), bf16(128, WIDE),
            *sums(CHUNK), *sums(HALF_CHUNK), *sums(HALF_CHUNK),
            f32(2, 56, 128), f32(2, 56, 128), f32(56, 128), f32(2, 56, 128), f32(2, 56, 128), f32(56, 128), f32(56, 128),
            f32(2, S, 128), f32(2, S, 128), f32(S, 128), f32(2, S, 128), f32(2, S, 128), f32(S, 128), f32(S, 128),
            pltpu.SemaphoreType.DMA((8,)), pltpu.SemaphoreType.DMA((8,)),
            pltpu.SemaphoreType.DMA((9,)), pltpu.SemaphoreType.DMA((9,)), pltpu.SemaphoreType.DMA((5,)),
        ],
        compiler_params=pltpu.CompilerParams(
            collective_id=0, has_side_effects=True, vmem_limit_bytes=32 * 1024 * 1024
        ),
    )(
        *(
            pltpu.with_memory_space_constraint(value, pltpu.MemorySpace.HBM)
            for value in (
                modes.reshape(S * 16, 128),
                mean_flow.reshape(16, 128),
                seeds.T,
                amplitudes.reshape(1, S),
                water_mask,
            )
        )
    )
    return new_modes.reshape(S, 2, 8, 128), new_coeffs.T


def solution(mesh):
    return jax.shard_map(
        on_device,
        mesh=mesh,
        in_specs=(
            P(None, None, "row", "col"),
            P(None, "row", "col"),
            P(("row", "col"), None),
            P(),
            P("row", "col"),
        ),
        out_specs=(P(None, None, "row", "col"), P(("row", "col"), None)),
        check_vma=False,
    )
```

```python
import math

import jax
import jax.numpy as jnp
from jax import lax
from jax.experimental import pallas as pl
from jax.experimental.pallas import tpu as pltpu
from jax.sharding import PartitionSpec as P

F32 = jnp.float32
BF16 = jnp.bfloat16
MESH = pl.DeviceIdType.MESH
HIGHEST = lax.Precision.HIGHEST

S = 48
R = 32768
CELLS = 2.0 * 64 * 4096
STEP = 0.25
VISCOUS = 0.2
ROWS, COLS, ALONG_X = 8, 32, 4
GROUP = ROWS * ALONG_X
DEEP = COLS // ALONG_X
CHUNK = 16
REGION = GROUP * CHUNK
HALF_CHUNK = CHUNK // 2
HALF_REGION = GROUP * HALF_CHUNK
PAIRS = 1176
WIDE = 1280
INNER = [(c, s) for s in range(1, 7) for c in range(2)]
OUTER = [(c, s) for s in (0, 7) for c in range(2)]
SLOT = {place: number for number, place in enumerate(INNER + OUTER)}
SEAM = 16
LANES = 18 * 128
NT = (((1,), (1,)), ((), ()))


def split(value):
    high = value.astype(BF16)
    return high, (value - high.astype(F32)).astype(BF16)


def dot(a, b):
    return jnp.dot(a, b, preferred_element_type=F32)


def dot_nt(a, b):
    return lax.dot_general(a, b, NT, preferred_element_type=F32)


def exact(a, b):
    return jnp.dot(a, b, precision=HIGHEST, preferred_element_type=F32)


def exact_nt(a, b):
    return lax.dot_general(a, b, NT, precision=HIGHEST, preferred_element_type=F32)


def tall(value):
    return jnp.concatenate([value, jnp.zeros((128 - S, 128), F32)], axis=0)


def kernel(
    modes_hbm, mean_hbm, seeds_hbm, amps_hbm, water_hbm, new_modes, new_coeffs,
    modes, mean, seeds, amps, water,
    base, both, grad_x, grad_y, back, weighted, pair_high, pair_low, side_high, side_low,
    seam_field, seam_slope, seam_back, amp_row, coeffs, pair_coeffs, moments, tensor_b, tensor_c, cube, cube_split, pair_cov,
    cov_inv, gram_inv, half, key_high, key_low,
    part_a, deep_a, mine_a, total_a, part_b, deep_b, mine_b, total_b, part_c, deep_c, mine_c, total_c,
    up_out, down_out, side_out, up_in, down_in, left_in, right_in,
    up_out2, down_out2, side_out2, up_in2, down_in2, left_in2, right_in2,
    halo_send, halo_recv, sum_send, sum_recv, fetch_sem,
):
    row = lax.axis_index("row")
    col = lax.axis_index("col")
    along_x = lax.rem(col, ALONG_X)
    plane = lax.div(col, ALONG_X)
    place = row * ALONG_X + along_x
    above = lax.rem(row + ROWS - 1, ROWS)
    below = lax.rem(row + 1, ROWS)
    left = lax.rem(col + COLS - 1, COLS)
    right = lax.rem(col + 1, COLS)

    def member(offset):
        other = lax.rem(place + offset, GROUP)
        return other, (lax.div(other, ALONG_X), plane * ALONG_X + lax.rem(other, ALONG_X))

    def deep(offset):
        return (row, lax.rem(plane + offset, DEEP) * ALONG_X + along_x)

    barrier = pltpu.get_barrier_semaphore()

    def greet_plane(offset, carry):
        pl.semaphore_signal(barrier, inc=1, device_id=member(offset)[1], device_id_type=MESH)
        return carry

    def greet_deep(offset, carry):
        pl.semaphore_signal(barrier, inc=1, device_id=deep(offset), device_id_type=MESH)
        return carry

    for offset in range(1, GROUP):
        greet_plane(offset, 0)
    for offset in range(1, DEEP):
        greet_deep(offset, 0)
    pl.semaphore_signal(barrier, inc=1, device_id=(row, left), device_id_type=MESH)
    pl.semaphore_signal(barrier, inc=1, device_id=(row, right), device_id_type=MESH)

    fetches = [
        pltpu.make_async_copy(source, target, fetch_sem.at[k])
        for k, (source, target) in enumerate(
            ((seeds_hbm, seeds), (amps_hbm, amps), (modes_hbm, modes), (mean_hbm, mean), (water_hbm, water))
        )
    ]
    for fetch in fetches:
        fetch.start()

    lane = lax.broadcasted_iota(jnp.int32, (S, 128), 1)
    lane1 = lax.broadcasted_iota(jnp.int32, (1, 128), 1)
    sub = lax.broadcasted_iota(jnp.int32, (S, 128), 0)
    sub8 = lax.broadcasted_iota(jnp.int32, (8, 128), 0)

    def copies(outs, ins, first):
        targets = ((above, col), (below, col), (row, left), (row, right))
        arrivals = (ins[1], ins[0], ins[3], ins[2])
        return [
            pltpu.make_async_remote_copy(
                src_ref=outs[k],
                dst_ref=arrivals[k],
                send_sem=halo_send.at[first + k],
                recv_sem=halo_recv.at[first + k],
                device_id=targets[k],
                device_id_type=MESH,
            )
            for k in range(4)
        ]

    def plane_start(source, parts, sems, chunk):
        def send(offset, carry):
            other, device = member(offset)
            pltpu.make_async_remote_copy(
                src_ref=source.at[pl.ds(pl.multiple_of(other * chunk, chunk), chunk)],
                dst_ref=parts.at[pl.ds(pl.multiple_of((offset - 1) * chunk, chunk), chunk)],
                send_sem=sum_send.at[sems],
                recv_sem=sum_recv.at[sems],
                device_id=device,
                device_id_type=MESH,
            ).start()
            return carry

        for offset in range(1, GROUP):
            send(offset, 0)

    def deep_start(source, parts, mine, deeper, sems, chunk):
        pltpu.make_async_copy(parts, parts, sum_recv.at[sems]).wait()
        value = source[pl.ds(pl.multiple_of(place * chunk, chunk), chunk), :]
        for k in range(GROUP - 1):
            value = value + parts[k * chunk : (k + 1) * chunk, :]
        mine[0:chunk, :] = value

        def send(offset, carry):
            pltpu.make_async_remote_copy(
                src_ref=mine.at[pl.ds(0, chunk)],
                dst_ref=deeper.at[pl.ds(pl.multiple_of((offset - 1) * chunk, chunk), chunk)],
                send_sem=sum_send.at[sems + 1],
                recv_sem=sum_recv.at[sems + 1],
                device_id=deep(offset),
                device_id_type=MESH,
            ).start()
            return carry

        for offset in range(1, DEEP):
            send(offset, 0)

    def gather_start(mine, deeper, total, sems, chunk):
        pltpu.make_async_copy(deeper, deeper, sum_recv.at[sems + 1]).wait()
        value = mine[0:chunk, :]
        for k in range(DEEP - 1):
            value = value + deeper[k * chunk : (k + 1) * chunk, :]
        mine[chunk : 2 * chunk, :] = value
        own = pl.ds(pl.multiple_of(place * chunk, chunk), chunk)
        total[own, :] = value

        def send(offset, carry):
            pltpu.make_async_remote_copy(
                src_ref=mine.at[pl.ds(chunk, chunk)],
                dst_ref=total.at[own],
                send_sem=sum_send.at[sems + 2],
                recv_sem=sum_recv.at[sems + 2],
                device_id=member(offset)[1],
                device_id_type=MESH,
            ).start()
            return carry

        for offset in range(1, GROUP):
            send(offset, 0)

    def gather_wait(parts, sems):
        pltpu.make_async_copy(parts, parts, sum_recv.at[sems + 2]).wait()

    def sums_sent(parts, deeper, sems):
        pltpu.make_async_copy(parts, parts, sum_send.at[sems]).wait()
        pltpu.make_async_copy(deeper, deeper, sum_send.at[sems + 1]).wait()
        pltpu.make_async_copy(parts, parts, sum_send.at[sems + 2]).wait()

    for fetch in fetches[:2]:
        fetch.wait()
    phase = seeds[...].astype(F32) * (3.0 * math.pi / 8192.0)
    wave = jnp.cos(phase)
    strength = 0.5 + ((row * COLS + col) * 128 + lane).astype(F32) * (1.0 / R)
    amp_row[...] = jnp.zeros((8, 128), F32)
    amp_row[0:1, 0:S] = amps[...]
    amp_col = jnp.sum(jnp.where(lane == sub, amp_row[0:1, :], 0.0), axis=1, keepdims=True)
    raw = strength * amp_col * (wave + (wave * wave - 0.5))

    def pair_up(values, ones):
        coeffs[0:S, :] = values
        coeffs[S : S + 24, :] = values[0:24]
        for d in range(24):
            pair_coeffs[d * S : (d + 1) * S, :] = values * coeffs[d : d + S, :]
        pair_coeffs[1152:PAIRS, :] = values[0:24] * coeffs[24:48, :]
        pair_coeffs[PAIRS : PAIRS + S, :] = values
        pair_coeffs[PAIRS + S : WIDE, :] = jnp.zeros((WIDE - PAIRS - S, 128), F32)
        if ones:
            pair_coeffs[1272:1280, :] = jnp.where(sub8 == 0, 1.0, 0.0)

    pair_up(raw, True)
    for lb in range(5):
        out = exact_nt(raw, pair_coeffs[lb * 256 : (lb + 1) * 256, :])
        moments[lb * 96 : lb * 96 + S, :] = out[:, 0:128]
        moments[lb * 96 + S : lb * 96 + 96, :] = out[:, 128:256]
    for fetch in fetches[2:]:
        fetch.wait()

    def lanes_of(c, s):
        return slice(SLOT[c, s] * 128, (SLOT[c, s] + 1) * 128)

    seam_lanes = slice(SEAM * 128, LANES)
    side_high[...] = jnp.zeros((128, LANES), BF16)
    side_low[...] = jnp.zeros((128, LANES), BF16)
    lane56 = lax.broadcasted_iota(jnp.int32, (56, 128), 1)
    columns = jnp.zeros((56, 128), F32)
    shore = jnp.zeros((1, 128), F32)
    for t in range(16):
        c, s = divmod(t, 8)
        field = modes[pl.ds(t, S, stride=16), :]
        drift_row = jnp.where(sub8 == 0, jnp.broadcast_to(mean[t : t + 1, :], (8, 128)), 0.0)
        block = jnp.concatenate([field, drift_row], axis=0)
        base[t] = block
        both[t, 0:S, :] = field
        both[t, S : S + 24, :] = field[0:24]
        weight = water[s : s + 1, :].astype(F32) * (-1.0 / CELLS)
        high, low = split(field * weight)
        weighted[0:S, lanes_of(c, s)] = high
        weighted[S : 2 * S, lanes_of(c, s)] = low
        high, low = split(field)
        side_high[64 : 64 + S, lanes_of(c, s)] = high
        side_low[64 : 64 + S, lanes_of(c, s)] = low
        columns = jnp.where(lane56 == 64 + t, pltpu.roll(block, 64 + t, 1), columns)
        columns = jnp.where(lane56 == t, pltpu.roll(block, t + 1, 1), columns)
        shore = jnp.where(lane1 == t, pltpu.roll(weight, t, 1) if t else weight, shore)
        shore = jnp.where(lane1 == 64 + t, pltpu.roll(weight, 65 + t, 1), shore)
        if s == 0:
            up_out[c] = block
        if s == 7:
            down_out[c] = block
        ahead = jnp.where(lane56 == 127, 0.0, pltpu.roll(block, 127, 1))
        behind = jnp.where(lane56 == 0, 0.0, pltpu.roll(block, 1, 1))
        across = 0.5 * (ahead - behind)
        grad_y[t, 0:S, :] = across[0:S]
        grad_y[t, S : S + 24, :] = across[0:24]
        grad_y[t, 72:80, :] = across[S:56]
    side_out[...] = columns

    def slope(t, before, after):
        along = 0.5 * (after - before)
        grad_x[t, 0:S, :] = along[0:S]
        grad_x[t, S : S + 24, :] = along[0:24]
        grad_x[t, 72:80, :] = along[S:56]

    for c, s in INNER:
        slope(c * 8 + s, base[c * 8 + s - 1], base[c * 8 + s + 1])

    own = pltpu.roll(columns, 64, 1)
    high, low = split(own[0:S] * shore)
    weighted[0:S, seam_lanes] = jnp.concatenate([high, jnp.zeros((S, 128), BF16)], axis=1)
    weighted[S : 2 * S, seam_lanes] = jnp.concatenate([low, jnp.zeros((S, 128), BF16)], axis=1)
    second_half = lax.rem(lax.div(lane56, 8), 2) == 1
    own = jnp.where(second_half, own, pltpu.roll(own, 120, 1))
    seam_field[0:S, :] = own[0:S]
    seam_field[S : S + 24, :] = own[0:24]
    seam_field[72:80, :] = own[S:56]

    gram = dot_nt(weighted[...], side_high[...])
    gram = gram[0:S] + gram[S : 2 * S] + dot_nt(weighted[0:S, :], side_low[...])
    moments[432:480, :] = moments[432:480, :] - pltpu.roll(gram, 8, 1)
    moments[480:REGION, :] = jnp.zeros((REGION - 480, 128), F32)
    pl.semaphore_wait(barrier, GROUP - 1 + DEEP - 1 + 2)
    halo = copies(
        (up_out, down_out, side_out, side_out), (up_in, down_in, left_in, right_in), 0
    )
    for copy in halo:
        copy.start()
    plane_start(moments, part_a, 0, CHUNK)

    def pair_value(d, t, u0, u1, v0, v1):
        ahead = pl.ds(d, S)
        return (
            u0 * grad_x[t, ahead, :] + u1 * grad_y[t, ahead, :]
            + v0 * grad_x[t, 0:S, :] + v1 * grad_y[t, 0:S, :]
        )

    def store(rows, lanes, value):
        high, low = split(value)
        pair_high[rows, lanes] = high
        pair_low[rows, lanes] = low

    def block_rows(d):
        return slice(d * S, (d + 1) * S) if isinstance(d, int) else pl.ds(pl.multiple_of(d * S, S), S)

    def pairs_of(grid_rows, together):
        def pair_block(first, carry):
            for s in grid_rows:
                u0, u1 = both[s, 0:S, :], both[8 + s, 0:S, :]
                slopes = [(grad_x[c * 8 + s, 0:S, :], grad_y[c * 8 + s, 0:S, :]) for c in range(2)]
                for k in range(together):
                    d = first + k
                    rows = block_rows(d)
                    ahead = pl.ds(d, S)
                    v0, v1 = both[s, ahead, :], both[8 + s, ahead, :]
                    for c in range(2):
                        t = c * 8 + s
                        value = (
                            u0 * grad_x[t, ahead, :] + u1 * grad_y[t, ahead, :]
                            + v0 * slopes[c][0] + v1 * slopes[c][1]
                        )
                        store(rows, lanes_of(c, s), value)
            return carry

        return pair_block

    def last_rows(lanes, value, minus):
        store(slice(1152, 1200), lanes, jnp.concatenate([value[0:24], minus[0:24]], axis=0))
        store(slice(1200, WIDE), lanes, jnp.concatenate([minus[24:48], jnp.zeros((56, 128), F32)], axis=0))

    def other_pairs(grid_rows):
        for s in grid_rows:
            u0, u1 = both[s, 0:S, :], both[8 + s, 0:S, :]
            v0, v1 = both[s, 24:72, :], both[8 + s, 24:72, :]
            m0, m1 = base[s, S : S + 1, :], base[8 + s, S : S + 1, :]
            for c in range(2):
                t = c * 8 + s
                store(slice(0, S), lanes_of(c, s), u0 * grad_x[t, 0:S, :] + u1 * grad_y[t, 0:S, :])
                minus = (
                    m0 * grad_x[t, 0:S, :] + m1 * grad_y[t, 0:S, :]
                    + u0 * grad_x[t, 72:73, :] + u1 * grad_y[t, 72:73, :]
                )
                back[t] = minus
                last_rows(lanes_of(c, s), pair_value(24, t, u0, u1, v0, v1), minus)

    def project(first, count, target):
        rows = slice(first, first + count)
        out = dot_nt(weighted[...], pair_high[rows, :])
        out = out[0:S] + out[S : 2 * S] + dot_nt(weighted[0:S, :], pair_low[rows, :])
        for k in range(count // 128):
            to = (first // 128 + k) % 5 * S
            target[to : to + S, :] = out[:, k * 128 : (k + 1) * 128]

    other_pairs(range(1, 7))
    pairs_of(range(1, 7), 1)(1, 0)
    lax.fori_loop(1, 12, lambda i, carry: pairs_of(range(1, 7), 2)(2 * i, carry), 0)

    for copy in halo[0:2]:
        copy.wait_recv()
    for c in range(2):
        slope(c * 8, jnp.where(row == 0, 0.0, up_in[c]), base[c * 8 + 1])
        slope(c * 8 + 7, base[c * 8 + 6], jnp.where(row == ROWS - 1, 0.0, down_in[c]))
    other_pairs((0, 7))
    pairs_of((0, 7), 1)(1, 0)
    for copy in halo[2:4]:
        copy.wait_recv()
    from_left = jnp.where(col == 0, 0.0, left_in[...])
    from_right = jnp.where(col == COLS - 1, 0.0, right_in[...])
    change = jnp.where(lane56 < 64, -0.5 * from_left, 0.5 * from_right)
    seam_slope[0:S, :] = change[0:S]
    seam_slope[S : S + 24, :] = change[0:24]
    seam_slope[72:80, :] = change[S:56]
    seam = slice(SEAM * 128, (SEAM + 1) * 128)

    def seam_value(d):
        ahead = pl.ds(d, S)
        return seam_field[0:S, :] * seam_slope[ahead, :] + seam_field[ahead, :] * seam_slope[0:S, :]

    def outer_pairs(i, carry):
        for k in range(2):
            store(block_rows(2 * i + k), seam, seam_value(2 * i + k))
        return pairs_of((0, 7), 2)(2 * i, carry)

    minus = seam_field[72:73, :] * seam_slope[0:S, :] + seam_field[0:S, :] * seam_slope[72:73, :]
    seam_back[...] = minus
    store(slice(0, S), seam, seam_field[0:S, :] * seam_slope[0:S, :])
    last_rows(seam, seam_value(24), minus)
    pair_high[:, 17 * 128 : LANES] = jnp.zeros((WIDE, 128), BF16)
    pair_low[:, 17 * 128 : LANES] = jnp.zeros((WIDE, 128), BF16)
    store(slice(S, 2 * S), seam, seam_value(1))
    lax.fori_loop(1, 7, outer_pairs, 0)
    project(0, 256, tensor_b)
    project(256, 256, tensor_b)
    project(512, 128, tensor_b)
    for i in range(7, 12):
        outer_pairs(i, 0)
    tensor_b[240:HALF_REGION, :] = jnp.zeros((HALF_REGION - 240, 128), F32)
    plane_start(tensor_b, part_b, 3, HALF_CHUNK)
    deep_start(moments, part_a, mine_a, deep_a, 0, CHUNK)

    project(640, 128, tensor_c)
    project(768, 256, tensor_c)
    project(1024, 256, tensor_c)
    tensor_c[240:HALF_REGION, :] = jnp.zeros((HALF_REGION - 240, 128), F32)
    plane_start(tensor_c, part_c, 6, HALF_CHUNK)
    deep_start(tensor_b, part_b, mine_b, deep_b, 3, HALF_CHUNK)
    gather_start(mine_a, deep_a, total_a, 0, CHUNK)
    deep_start(tensor_c, part_c, mine_c, deep_c, 6, HALF_CHUNK)

    gather_start(mine_b, deep_b, total_b, 3, HALF_CHUNK)
    gather_start(mine_c, deep_c, total_c, 6, HALF_CHUNK)
    gather_wait(part_a, 0)
    tail = total_a[432:480, :]
    second = jnp.where(lane < S, pltpu.roll(tail, 128 - 24, 1), 0.0) * (1.0 / R)
    gram_inv[...] = jnp.where(lane < S, pltpu.roll(tail, 128 - 72, 1), 0.0)
    mean_col = jnp.sum(jnp.where(lane == 120, tail, 0.0), axis=1, keepdims=True) * (1.0 / R)
    mean_row = jnp.sum(jnp.where(lane == sub, mean_col, 0.0), axis=0, keepdims=True)
    cov_inv[...] = second - mean_col * mean_row
    def split3(value):
        high, low = split(value)
        lowest = (value - high.astype(F32) - low.astype(F32)).astype(BF16)
        return jnp.concatenate([high, low, lowest], axis=0)

    spread = split3(second)
    for lb in range(10):
        number = lb * 128 + lane
        first_d = lb * 128 // S
        d = jnp.full((S, 128), first_d, jnp.int32)
        for step in range(first_d + 1, first_d + 4):
            d = d + jnp.where(number >= step * S, 1, 0)
        k = number - d * S
        l = k + d
        l = jnp.where(l >= S, l - S, l)
        hot_k = jnp.where(sub == k, 1.0, 0.0)
        hot_l = jnp.where(sub == l, 1.0, 0.0)
        hot = jnp.concatenate([tall(hot_k), tall(hot_l)], axis=1).astype(BF16)
        out = dot(spread, hot)
        out = out[0:S] + out[S : 2 * S] + out[2 * S : 3 * S]
        at_k, at_l = out[:, 0:128], out[:, 128:256]
        mean_k = jnp.sum(mean_col * hot_k, axis=0, keepdims=True)
        mean_l = jnp.sum(mean_col * hot_l, axis=0, keepdims=True)
        second_kl = jnp.sum(hot_k * at_l, axis=0, keepdims=True)
        third = total_a[lb * S : (lb + 1) * S, :] * (1.0 / R)
        third = third - mean_col * (second_kl - 2.0 * (mean_k * mean_l)) - mean_k * at_l - mean_l * at_k
        cov = second_kl - mean_k * mean_l
        if lb == 9:
            third = jnp.where(lane < 24, third, 0.0)
            cov = jnp.where(lane1 < 24, cov, 0.0)
        cube[lb * S : (lb + 1) * S, :] = third
        high, low = split(third)
        cube_split[0:S, lb * 128 : (lb + 1) * 128] = high
        cube_split[S : 2 * S, lb * 128 : (lb + 1) * 128] = low
        pair_cov[lb : lb + 1, :] = cov

    def contract(n, carry):
        cells = pl.ds(pl.multiple_of(n * 256, 256), 256)
        out = dot(cube_split[...], pair_high[:, cells])
        out = out[0:S] + out[S : 2 * S] + dot(cube_split[0:S, :], pair_low[:, cells])
        high, low = split(out)
        side_high[0:S, cells] = high
        side_low[0:S, cells] = low
        return carry

    def picked(at, values, axis):
        return jnp.sum(jnp.where(at, values, 0.0), axis=axis, keepdims=True)

    def eliminate(i, carry):
        p = 2 * i
        for matrix in (cov_inv, gram_inv):
            value = matrix[...]
            line_p, line_q = matrix[pl.ds(p, 1), :], matrix[pl.ds(p + 1, 1), :]
            at_p, at_q = lane1 == p, lane1 == p + 1
            a, b, d = picked(at_p, line_p, 1), picked(at_q, line_p, 1), picked(at_q, line_q, 1)
            column_p, column_q = picked(lane == p, value, 1), picked(lane == p + 1, value, 1)
            inverse = 1.0 / a
            ratio = b * inverse
            g = 1.0 / (d - b * ratio)
            f = -ratio * g
            e = inverse - ratio * f
            new_p = jnp.where(at_p, e, jnp.where(at_q, f, e * line_p + f * line_q))
            new_q = jnp.where(at_p, f, jnp.where(at_q, g, f * line_p + g * line_q))
            value = jnp.where((lane == p) | (lane == p + 1), 0.0, value)
            value = value - column_p * new_p - column_q * new_q
            matrix[...] = jnp.where(sub == p, new_p, jnp.where(sub == p + 1, new_q, value))
        return carry

    def contract_and_eliminate(n, carry):
        contract(n, carry)
        for k in range(3):
            eliminate(n * 3 + k, carry)
        return carry

    lax.fori_loop(0, 8, contract_and_eliminate, 0)
    contract(8, 0)

    from_cov = split3(cov_inv[...])
    from_gram = split3(pltpu.roll(gram_inv[...], 64, 1))
    out = dot(from_cov[:, 0:S], cube_split[0:S, :])
    rest = dot(from_cov[0 : 2 * S, 0:S], cube_split[S : 2 * S, :])
    keys = out[0:S] + out[S : 2 * S] + out[2 * S : 3 * S] + rest[0:S] + rest[S : 2 * S]
    for lb in range(10):
        value = keys[:, lb * 128 : (lb + 1) * 128]
        if lb == 9:
            value = jnp.where(lane == sub + 24, 1.0, value)
        high, low = split(value)
        key_high[0:S, lb * 128 : (lb + 1) * 128] = high
        key_low[0:S, lb * 128 : (lb + 1) * 128] = low
    key_high[S:128, :] = jnp.zeros((128 - S, WIDE), BF16)
    key_low[S:128, :] = jnp.zeros((128 - S, WIDE), BF16)

    def product(factors, cells):
        out = dot(factors, side_high[:, cells])
        rest = dot(factors[0 : 2 * S], side_low[:, cells])
        return out[0:S] + out[S : 2 * S] + out[2 * S : 3 * S] + rest[0:S] + rest[S : 2 * S]

    seam_part = product(from_cov, slice(2048, LANES))[:, 0:128] + seam_back[...]
    for n in range(8):
        cells = slice(n * 256, (n + 1) * 256)
        out = product(from_cov, cells)
        high, low = split(product(from_gram, cells))
        side_high[64 : 64 + S, cells] = high
        side_low[64 : 64 + S, cells] = low
        for k in range(2):
            c, s = (INNER + OUTER)[2 * n + k]
            t = c * 8 + s
            part = back[t] + out[:, k * 128 : (k + 1) * 128]
            at_left = pltpu.roll(seam_part, 128 - t, 1) if t else seam_part
            part = part + jnp.where(lane == 0, at_left, 0.0)
            part = part + jnp.where(lane == 127, pltpu.roll(seam_part, 63 - t, 1), 0.0)
            half[t] = both[t, 0:S, :] - STEP * part
    gather_wait(part_b, 3)
    gather_wait(part_c, 6)

    def summed(lb):
        return (total_b if lb < 5 else total_c)[lb % 5 * S : (lb % 5 + 1) * S, :]

    totals = split3(jnp.concatenate([summed(lb) for lb in range(10)], axis=1))
    out = dot_nt(totals, key_high[...])
    rest = dot_nt(totals[0 : 2 * S], key_low[...])
    out = out[0:S] + out[S : 2 * S] + out[2 * S : 3 * S] + rest[0:S] + rest[S : 2 * S]
    from_sums = split3(pltpu.roll(tall(out).T[0:S], 64, 1))
    halo2 = copies(
        (up_out2, down_out2, side_out2, side_out2), (up_in2, down_in2, left_in2, right_in2), 4
    )
    columns = jnp.zeros((S, 128), F32)
    for n in (6, 7, 0, 1, 2, 3, 4, 5):
        out = product(from_sums, slice(n * 256, (n + 1) * 256))
        for k in range(2):
            c, s = (INNER + OUTER)[2 * n + k]
            t = c * 8 + s
            value = half[t] - STEP * out[:, k * 128 : (k + 1) * 128]
            value = water[s : s + 1, :].astype(F32) * value
            half[t] = value
            columns = jnp.where(lane == 64 + t, pltpu.roll(value, 64 + t, 1), columns)
            columns = jnp.where(lane == t, pltpu.roll(value, t + 1, 1), columns)
            if s == 0:
                up_out2[c] = value
            if s == 7:
                down_out2[c] = value
        if n == 7:
            for copy in halo2[0:2]:
                copy.start()
    side_out2[...] = columns
    for copy in halo2[2:4]:
        copy.start()

    centred = raw - mean_col
    pair_up(centred, False)
    change = jnp.zeros((S, 128), F32)
    excess = jnp.zeros((S, 128), F32)
    for lb in range(10):
        here = summed(lb)
        change = change + exact(here, pair_coeffs[lb * 128 : (lb + 1) * 128, :])
        excess = excess + here * pair_cov[lb : lb + 1, :]
    change = change - jnp.sum(excess, axis=1, keepdims=True)
    new_coeffs[...] = centred + STEP * exact(gram_inv[...], tall(change))

    for copy in halo2:
        copy.wait_recv()
    from_left = jnp.where(col == 0, 0.0, left_in2[...])
    from_right = jnp.where(col == COLS - 1, 0.0, right_in2[...])
    for t in range(16):
        c, s = divmod(t, 8)
        value = half[t]
        before = jnp.where(row == 0, 0.0, up_in2[c]) if s == 0 else half[t - 1]
        after = jnp.where(row == ROWS - 1, 0.0, down_in2[c]) if s == 7 else half[t + 1]
        ahead = jnp.where(lane == 127, pltpu.roll(from_right, 63 - t, 1), pltpu.roll(value, 127, 1))
        shifted = pltpu.roll(from_left, 128 - t, 1) if t else from_left
        behind = jnp.where(lane == 0, shifted, pltpu.roll(value, 1, 1))
        laplace = after + before + ahead + behind - 4.0 * value
        mask = water[s : s + 1, :].astype(F32)
        new_modes[pl.ds(t, S, stride=16), :] = mask * (value + VISCOUS * laplace)

    for copy in halo + halo2:
        copy.wait_send()
    sums_sent(part_a, deep_a, 0)
    sums_sent(part_b, deep_b, 3)
    sums_sent(part_c, deep_c, 6)


def on_device(modes, mean_flow, seeds, amplitudes, water_mask):
    vmem = pl.BlockSpec(memory_space=pltpu.VMEM)

    def f32(*shape):
        return pltpu.VMEM(shape, F32)

    def bf16(*shape):
        return pltpu.VMEM(shape, BF16)

    def sums(chunk):
        return [
            f32((GROUP - 1) * chunk, 128), f32((DEEP - 1) * chunk, 128), f32(2 * chunk, 128), f32(GROUP * chunk, 128)
        ]

    new_modes, new_coeffs = pl.pallas_call(
        kernel,
        out_shape=(
            jax.ShapeDtypeStruct((S * 16, 128), F32),
            jax.ShapeDtypeStruct((S, 128), F32),
        ),
        in_specs=[pl.BlockSpec(memory_space=pltpu.MemorySpace.HBM)] * 5,
        out_specs=(vmem, vmem),
        scratch_shapes=[
            f32(S * 16, 128), f32(16, 128), pltpu.VMEM((S, 128), jnp.int32), f32(1, S), pltpu.VMEM((8, 128), jnp.int32),
            f32(16, 56, 128), f32(16, 72, 128), f32(16, 80, 128), f32(16, 80, 128), f32(16, S, 128),
            bf16(2 * S, LANES), bf16(WIDE, LANES), bf16(WIDE, LANES), bf16(128, LANES), bf16(128, LANES),
            f32(80, 128), f32(80, 128), f32(S, 128), f32(8, 128), f32(72, 128), f32(WIDE, 128),
            f32(REGION, 128), f32(HALF_REGION, 128), f32(HALF_REGION, 128), f32(480, 128), bf16(2 * S, WIDE),
            f32(16, 128), f32(S, 128), f32(S, 128), f32(16, S, 128), bf16(128, WIDE), bf16(128, WIDE),
            *sums(CHUNK), *sums(HALF_CHUNK), *sums(HALF_CHUNK),
            f32(2, 56, 128), f32(2, 56, 128), f32(56, 128), f32(2, 56, 128), f32(2, 56, 128), f32(56, 128), f32(56, 128),
            f32(2, S, 128), f32(2, S, 128), f32(S, 128), f32(2, S, 128), f32(2, S, 128), f32(S, 128), f32(S, 128),
            pltpu.SemaphoreType.DMA((8,)), pltpu.SemaphoreType.DMA((8,)),
            pltpu.SemaphoreType.DMA((9,)), pltpu.SemaphoreType.DMA((9,)), pltpu.SemaphoreType.DMA((5,)),
        ],
        compiler_params=pltpu.CompilerParams(
            collective_id=0, has_side_effects=True, vmem_limit_bytes=32 * 1024 * 1024
        ),
    )(
        *(
            pltpu.with_memory_space_constraint(value, pltpu.MemorySpace.HBM)
            for value in (
                modes.reshape(S * 16, 128),
                mean_flow.reshape(16, 128),
                seeds.T,
                amplitudes.reshape(1, S),
                water_mask,
            )
        )
    )
    return new_modes.reshape(S, 2, 8, 128), new_coeffs.T


def solution(mesh):
    return jax.shard_map(
        on_device,
        mesh=mesh,
        in_specs=(
            P(None, None, "row", "col"),
            P(None, "row", "col"),
            P(("row", "col"), None),
            P(),
            P("row", "col"),
        ),
        out_specs=(P(None, None, "row", "col"), P(("row", "col"), None)),
        check_vma=False,
    )
```
